32 devices in a mesh: dom: 8 (over z, y), ka: 4 (over x, core).
Axes of the slice: x: 2, y: 2, z: 4, core: 2. Of those that a mesh axis runs over, the one named last changes fastest.
Arguments:
- x_blocks: bfloat16 [64, 64, 2048], P('dom', None, 'ka'), may hold values from -0.29882812 to 0.29882812
- col_index: int32 [64, 32], P('dom'), may hold values from 0 to 63, as said below
- prod_index: int32 [64, 32], P('dom'), may hold values from 0 to 63, as said below
Outputs:
- purified: bfloat16 [64, 64, 2048], P('dom', None, 'ka')
The draws below stay inside these ranges and needn't reach their ends.
Inputs may be any that keep to these rules, and one draw needn't show every extreme that they name: `col_index`: row i lists 32 distinct block columns (i + o) mod 64 with offsets o between -16 and 16, in ascending order of o; the offsets 0, -16 and 16 are always among them. `prod_index`: row i lists 32 distinct block columns (i + o) mod 64 with offsets o between -16 and 16, in ascending order of o; the offsets 0, -16 and 16 are always among them.
All inputs are finite; a program needn't handle non-finite values.
Results may differ from the reference program's by a relative error of at most 0.013.
Values may be sent and summed in bfloat16 or wider, within the bound.
No kernel may reach another device: no remote copies, remote signals or barrier semaphores. Data moves between devices by JAX's collectives and lax.ppermute only.
A program may use at most 128 MiB of HBM per device.

```python
import jax
import jax.numpy as jnp
from jax import lax

B = 64
NNZ = 32
PNZ = 32
REACH = 16
NB = 64
N_KA = 4


def window_offsets(key, row_count, slot_count, reach_rows):
    span_width = 2 * reach_rows + 1
    scores = jax.random.randint(key, (row_count, span_width), 0, 1 << 20)
    position = jnp.arange(span_width, dtype=jnp.int32)[None, :]
    scores = scores * span_width + position
    forced = (position == 0) | (position == reach_rows) | (position == span_width - 1)
    scores = jnp.where(forced, (1 << 30) + position, scores)
    chosen = lax.top_k(scores, slot_count)[1].astype(jnp.int32)
    return jnp.sort(chosen, axis=1) - reach_rows


def columns_from(key, slot_count):
    offsets = window_offsets(key, NB, slot_count, REACH)
    rows_global = jnp.arange(NB, dtype=jnp.int32)[:, None]
    return (rows_global + offsets) % NB


def draw_col_index(key, part):
    return columns_from(jax.random.fold_in(key, 17), NNZ)


def draw_prod_index(key, part):
    return columns_from(jax.random.fold_in(key, 29), PNZ)


def block_scale(rng, dims, split, least, top_value):
    factor_of = 1.0
    for axis_at, shards_of in split:
        steps = jax.random.uniform(jax.random.fold_in(jax.random.fold_in(rng, 6), axis_at), (shards_of,), jnp.float32, least / len(split), top_value / len(split))
        factor_of = factor_of * jnp.repeat(jnp.exp(steps), dims[axis_at] // shards_of).reshape((-1,) + (1,) * (len(dims) - 1 - axis_at))
    return factor_of


def noise(own_key, shape, scale, most, cuts=(), kind=jnp.bfloat16):
    array = scale * jax.random.normal(own_key, shape, jnp.float32)
    if cuts:
        array = array * block_scale(own_key, shape, cuts, -0.22, 0.18)
    return jnp.clip(array, -most, most).astype(kind)


def setup_inputs(seed: int = 0) -> dict:
    splits = jax.random.split(jax.random.key(seed), 4)
    return {
        "x_blocks": noise(splits[0], (NB, B, NNZ * B), 0.05, 0.29882812, ((0, 8), (2, 4))),
        "col_index": draw_col_index(jax.random.fold_in(splits[3], 71), 0),
        "prod_index": draw_prod_index(jax.random.fold_in(splits[3], 71), 0),
    }


def block_table(blocks, columns, left_columns, target_columns):
    row_columns = jnp.take(columns, left_columns, axis=0)
    matches = row_columns[:, None, :] == target_columns[None, :, None]
    present = jnp.any(matches, axis=2)
    slot_index = jnp.argmax(matches, axis=2).astype(jnp.int32)
    picked = blocks[left_columns[:, None], :, slot_index, :]
    return jnp.where(present[:, :, None, None], picked, jnp.zeros((), picked.dtype))


def grouped_sum(left_blocks, gathered, group_count):
    span_width = left_blocks.shape[1] // group_count
    summed = jnp.zeros((left_blocks.shape[0], gathered.shape[1], left_blocks.shape[2]), jnp.float32)
    for group_number in range(group_count):
        first = group_number * span_width
        partial_sum = jnp.einsum("asb,stbc->atc", left_blocks[:, first:first + span_width].astype(jnp.float32), gathered[first:first + span_width].astype(jnp.float32))
        rounded = lax.optimization_barrier(partial_sum.astype(jnp.bfloat16))
        summed = summed + rounded.astype(jnp.float32)
    return summed


def reference(x_blocks, col_index, prod_index):
    blocks = x_blocks.reshape(NB, B, NNZ, B)

    def one_row(row_index):
        left_columns = col_index[row_index]
        targets = prod_index[row_index]
        first_table = block_table(blocks, col_index, left_columns, targets)
        square = grouped_sum(blocks[row_index], first_table, N_KA)
        square_low = lax.optimization_barrier(square.astype(jnp.bfloat16))
        second_table = block_table(blocks, col_index, targets, targets)
        cube = grouped_sum(square_low, second_table, N_KA)
        return (3.0 * square - 2.0 * cube).astype(jnp.bfloat16).reshape(B, PNZ * B)

    return lax.map(one_row, jnp.arange(NB, dtype=jnp.int32))
```

```python
import functools

import jax
import jax.numpy as jnp
from jax import lax
from jax.experimental import pallas as pl
from jax.experimental.pallas import tpu as pltpu
from jax.sharding import PartitionSpec as P

CHUNKS = 1
WINDOWS = 5
PIECES = 3


def permuted(value, pairs):
    return lax.ppermute(value, ("dom", "ka"), pairs)


def routes(dom_count, ka_count):
    def pairs(target):
        out = []
        for dom in range(dom_count):
            for group in range(ka_count):
                to = target(dom, group, group // 2, dom % 2)
                if to is not None:
                    out.append((dom * ka_count + group, (to[0] % dom_count) * ka_count + to[1]))
        return out

    return {
        "za": pairs(lambda d, g, x, y: (d + 2 if x else d - 2, g)),
        "zb": pairs(lambda d, g, x, y: (d - 2 if x else d + 2, g)),
        "x": pairs(lambda d, g, x, y: (d, g ^ 2)),
        "y": pairs(lambda d, g, x, y: (d ^ 1, g)),
        "y_same": pairs(lambda d, g, x, y: (d ^ 1, g) if x == y else None),
        "y_other": pairs(lambda d, g, x, y: (d ^ 1, g) if x != y else None),
        "d_same": pairs(lambda d, g, x, y: (d ^ 1, g ^ 2) if x == y else None),
        "d_other": pairs(lambda d, g, x, y: (d ^ 1, g ^ 2) if x != y else None),
        "core": pairs(lambda d, g, x, y: (d, g ^ 1)),
        "core_za": pairs(lambda d, g, x, y: (d, g ^ 1) if g in (0, 3) else None),
        "core_zb": pairs(lambda d, g, x, y: (d, g ^ 1) if g in (1, 2) else None),
    }


def shifted(wide, first, count):
    return wide[:, first:first + count]


def spread(pieces, shift, width, threshold):
    wide = jnp.concatenate(pieces, axis=1)
    low = shifted(wide, shift * 64, width * 64)
    high = shifted(wide, (shift - 1) * 64, width * 64)
    place = lax.broadcasted_iota(jnp.int32, low.shape, 1)
    zero = jnp.zeros_like(low)
    return jnp.where(place < threshold * 64, low, jnp.where(place >= threshold * 64 + 64, high, zero))


def kept(total, row, threshold, width):
    low = shifted(total, row * 64, width)
    high = shifted(total, (row + 1) * 64, width)
    place = lax.broadcasted_iota(jnp.int32, low.shape, 1)
    return jnp.where(place < threshold * 64, low, high)


def fill_left(left_ref, rows_of, thresholds, row_count):
    for row in range(row_count):
        blocks = rows_of(row)
        pad = jnp.zeros((64, 512), blocks[0].dtype)
        left_ref[row * 64:(row + 1) * 64, :] = spread(
            [pad] + blocks + [pad], 8 - row, WINDOWS * 8, thresholds(row)
        )


def product(left_ref, table_ref, total_ref):
    def step(tile, carry):
        cols = pl.ds(pl.multiple_of(tile * 256, 256), 256)
        total_ref[:, cols] = jnp.dot(left_ref[...], table_ref[:, cols], preferred_element_type=jnp.float32)
        return carry

    lax.fori_loop(0, table_ref.shape[1] // 256, step, 0)


def square_kernel(item_count, chunk_rows, meta_ref, *refs):
    items = refs[:item_count]
    table_ref, square_ref, low_ref = refs[item_count:item_count + 3]
    store, left_store, left_ref, total_ref, sems, left_sems = refs[item_count + 3:]
    row_count = square_ref.shape[0]
    base = 0
    dest_at = 65
    left_at = 65 + item_count
    valid_at = 65 + 2 * item_count

    def copies(number):
        rows = pl.ds((number % CHUNKS) * chunk_rows, chunk_rows)
        dest = meta_ref[dest_at + number]
        left = meta_ref[left_at + number]
        main = pltpu.make_async_copy(items[number], store.at[jnp.maximum(dest, 0), rows], sems.at[number])
        side = pltpu.make_async_copy(items[number], left_store.at[jnp.maximum(left, 0), rows], left_sems.at[number])
        return dest, left, main, side

    for number in range(item_count):
        dest, left, main, side = copies(number)
        pl.when(dest >= 0)(main.start)
        pl.when(left >= 0)(side.start)
    for place in range(WINDOWS * PIECES):
        @pl.when(meta_ref[valid_at + place] == 0)
        def _():
            store[place] = jnp.zeros(store.shape[1:], store.dtype)
    for number in range(item_count):
        dest, left, main, side = copies(number)
        pl.when(dest >= 0)(main.wait)
        pl.when(left >= 0)(side.wait)

    fill_left(left_ref, lambda row: [left_store[h, row] for h in range(4)], lambda row: meta_ref[40 + row], row_count)

    def window(delta, carry):
        for row in range(row_count):
            blocks = [store[delta * PIECES + piece, row] for piece in range(PIECES)]
            at = pl.ds(pl.multiple_of(delta * 512 + row * 64, 64), 64)
            table_ref[at, :] = spread(blocks, 8 - row, 16, meta_ref[base + delta * 8 + row])
        return carry

    lax.fori_loop(0, WINDOWS, window, 0)
    product(left_ref, table_ref, total_ref)
    for row in range(row_count):
        picked = kept(total_ref[row * 64:(row + 1) * 64, :], row, meta_ref[48 + row], 512)
        square_ref[row] = picked
        low_ref[row] = picked.astype(low_ref.dtype)


def cube_kernel(meta_ref, own_ref, core_ref, x_ref, far_ref, table_ref, square_ref, out_ref, store, left_ref, total_ref):
    row_count = out_ref.shape[0]
    group = meta_ref[64]
    for bits, ref in enumerate((own_ref, core_ref, x_ref, far_ref)):
        store[group ^ bits] = ref[...]
    fill_left(left_ref, lambda row: [store[h, row] for h in range(4)], lambda row: meta_ref[56 + row], row_count)
    product(left_ref, table_ref, total_ref)
    for row in range(row_count):
        cube = kept(total_ref[row * 64:(row + 1) * 64, :], row, meta_ref[48 + row], 512)
        out_ref[row] = (3.0 * square_ref[row] - 2.0 * cube).astype(out_ref.dtype)


def missing_places(index, rows, total_rows, reach):
    places = (index - rows[:, None] + reach) % total_rows
    slots = jnp.arange(index.shape[1], dtype=jnp.int32)[None, :]
    return jnp.sum((places == slots).astype(jnp.int32), axis=1)


def per_device(dom_count, ka_count, x_blocks, col_index, prod_index):
    row_count, block, width = x_blocks.shape
    reach = 2 * row_count
    total_rows = row_count * dom_count
    dom = lax.axis_index("dom")
    group = lax.axis_index("ka")
    x_side, y_side = group // 2, dom % 2
    route = routes(dom_count, ka_count)
    steps = jnp.arange(row_count, dtype=jnp.int32)
    rows = dom * row_count + steps
    col_missing = missing_places(col_index, rows, total_rows, reach)
    prod_missing = missing_places(prod_index, rows, total_rows, reach)

    def along(value, distance):
        return lax.ppermute(value, "dom", [(d, (d - distance) % dom_count) for d in range(dom_count)])

    missing = [col_missing if delta == 0 else along(col_missing, delta) for delta in range(-2, 3)]

    sign = 2 * x_side - 1
    same = x_side == y_side
    chunk_rows = row_count // CHUNKS
    kinds = {}

    def add(name, chunk, array, delta, held, valid):
        kinds.setdefault(name, []).append((array, delta, held, valid))

    for chunk in range(CHUNKS):
        own = x_blocks[chunk * chunk_rows:(chunk + 1) * chunk_rows]
        za = permuted(own, route["za"])
        zb = permuted(own, route["zb"])
        ox = permuted(own, route["x"])
        oy = permuted(own, route["y"])
        do = permuted(own, route["d_other"])
        bx = permuted(za, route["x"])
        by_a = permuted(za, route["y_same"])
        by_b = permuted(zb, route["y_other"])
        da = permuted(za, route["d_same"])
        near = 1 - 2 * y_side
        far = -near
        held = (
            ("own", own, 0, group, True, "core"),
            ("za", za, -2 * sign, group, True, "core_za"),
            ("zb", zb, 2 * sign, group, True, "core_zb"),
            ("ox", ox, 0, group ^ 2, True, "core"),
            ("oy", oy, near, group, True, "core"),
            ("do", do, sign, group ^ 2, jnp.logical_not(same), "core"),
            ("bx", bx, 2 * sign, group ^ 2, True, "core"),
            ("by_a", by_a, far, group, jnp.logical_not(same), "core"),
            ("by_b", by_b, far, group, same, "core"),
            ("da", da, sign, group ^ 2, same, "core"),
        )
        for name, array, delta, shard, valid, core_route in held:
            add(name, chunk, array, delta, shard, valid)
            valid_core = valid
            if core_route == "core_za":
                valid_core = (group == 1) | (group == 2)
            if core_route == "core_zb":
                valid_core = (group == 0) | (group == 3)
            add(name + "_core", chunk, permuted(array, route[core_route]), delta, shard ^ 1, valid_core)

    items, dests, lefts = [], [], []
    for entries in kinds.values():
        for array, delta, shard, valid in entries:
            piece = shard - group + delta + 1
            dest = (delta + 2) * PIECES + piece
            dests.append(jnp.where(valid & (piece >= 0) & (piece < PIECES), dest, -1))
            lefts.append(jnp.where(valid & (jnp.asarray(delta) == 0), shard, -1))
            items.append(array)
    valid_places = []
    for delta in range(-2, 3):
        for piece in range(PIECES):
            shard = group - delta - 1 + piece
            valid_places.append(((shard >= 0) & (shard < ka_count)).astype(jnp.int32))
    table_places = [
        missing[delta + 2] - 8 * (group - delta) + steps for delta in range(-2, 3)
    ]
    meta = jnp.concatenate(
        table_places
        + [col_missing + steps, prod_missing - 8 * group, prod_missing + steps, group[None]]
        + [jnp.stack(dests), jnp.stack(lefts), jnp.stack(valid_places)]
    ).astype(jnp.int32)

    smem = pl.BlockSpec(memory_space=pltpu.SMEM)
    vmem = pl.BlockSpec(memory_space=pltpu.VMEM)
    anywhere = pl.BlockSpec(memory_space=pl.ANY)
    depth = WINDOWS * 8 * block
    table, square, low = pl.pallas_call(
        functools.partial(square_kernel, len(items), chunk_rows),
        out_shape=(
            jax.ShapeDtypeStruct((depth, 16 * block), jnp.bfloat16),
            jax.ShapeDtypeStruct((row_count, block, width), jnp.float32),
            jax.ShapeDtypeStruct((row_count, block, width), jnp.bfloat16),
        ),
        in_specs=[smem] + [anywhere] * len(items),
        out_specs=(vmem, vmem, vmem),
        scratch_shapes=[
            pltpu.VMEM((WINDOWS * PIECES, row_count, block, width), jnp.bfloat16),
            pltpu.VMEM((ka_count, row_count, block, width), jnp.bfloat16),
            pltpu.VMEM((row_count * block, depth), jnp.bfloat16),
            pltpu.VMEM((row_count * block, 16 * block), jnp.float32),
            pltpu.SemaphoreType.DMA((len(items),)),
            pltpu.SemaphoreType.DMA((len(items),)),
        ],
    )(meta, *items)
    low_core = permuted(low, route["core"])
    low_x = permuted(low, route["x"])
    low_far = permuted(low_x, route["core"])
    return pl.pallas_call(
        cube_kernel,
        out_shape=jax.ShapeDtypeStruct((row_count, block, width), jnp.bfloat16),
        in_specs=[smem] + [vmem] * 6,
        out_specs=vmem,
        scratch_shapes=[
            pltpu.VMEM((ka_count, row_count, block, width), jnp.bfloat16),
            pltpu.VMEM((row_count * block, depth), jnp.bfloat16),
            pltpu.VMEM((row_count * block, 16 * block), jnp.float32),
        ],
    )(meta, low, low_core, low_x, low_far, table, square)


def solution(mesh):
    return jax.shard_map(
        functools.partial(per_device, mesh.shape["dom"], mesh.shape["ka"]),
        mesh=mesh,
        in_specs=(P("dom", None, "ka"), P("dom", None), P("dom", None)),
        out_specs=P("dom", None, "ka"),
        check_vma=False,
    )
```

```python
import functools

import jax
import jax.numpy as jnp
from jax import lax
from jax.experimental import pallas as pl
from jax.experimental.pallas import tpu as pltpu
from jax.sharding import PartitionSpec as P

CHUNKS = 1
WINDOWS = 5
PIECES = 3


def permuted(value, pairs):
    return lax.ppermute(value, ("dom", "ka"), pairs)


def routes(dom_count, ka_count):
    def pairs(target):
        out = []
        for dom in range(dom_count):
            for group in range(ka_count):
                to = target(dom, group, group // 2, dom % 2)
                if to is not None:
                    out.append((dom * ka_count + group, (to[0] % dom_count) * ka_count + to[1]))
        return out

    return {
        "za": pairs(lambda d, g, x, y: (d + 2 if x else d - 2, g)),
        "zb": pairs(lambda d, g, x, y: (d - 2 if x else d + 2, g)),
        "x": pairs(lambda d, g, x, y: (d, g ^ 2)),
        "y": pairs(lambda d, g, x, y: (d ^ 1, g)),
        "y_same": pairs(lambda d, g, x, y: (d ^ 1, g) if x == y else None),
        "y_other": pairs(lambda d, g, x, y: (d ^ 1, g) if x != y else None),
        "d_same": pairs(lambda d, g, x, y: (d ^ 1, g ^ 2) if x == y else None),
        "d_other": pairs(lambda d, g, x, y: (d ^ 1, g ^ 2) if x != y else None),
        "core": pairs(lambda d, g, x, y: (d, g ^ 1)),
        "core_za": pairs(lambda d, g, x, y: (d, g ^ 1) if g in (0, 3) else None),
        "core_zb": pairs(lambda d, g, x, y: (d, g ^ 1) if g in (1, 2) else None),
    }


def shifted(wide, first, count):
    return wide[:, first:first + count]


def spread(pieces, shift, width, threshold):
    wide = jnp.concatenate(pieces, axis=1)
    low = shifted(wide, shift * 64, width * 64)
    high = shifted(wide, (shift - 1) * 64, width * 64)
    place = lax.broadcasted_iota(jnp.int32, low.shape, 1)
    zero = jnp.zeros_like(low)
    return jnp.where(place < threshold * 64, low, jnp.where(place >= threshold * 64 + 64, high, zero))


def kept(total, row, threshold, width):
    low = shifted(total, row * 64, width)
    high = shifted(total, (row + 1) * 64, width)
    place = lax.broadcasted_iota(jnp.int32, low.shape, 1)
    return jnp.where(place < threshold * 64, low, high)


def fill_left(left_ref, rows_of, thresholds, row_count):
    for row in range(row_count):
        blocks = rows_of(row)
        pad = jnp.zeros((64, 512), blocks[0].dtype)
        left_ref[row * 64:(row + 1) * 64, :] = spread(
            [pad] + blocks + [pad], 8 - row, WINDOWS * 8, thresholds(row)
        )


def product(left_ref, table_ref, total_ref):
    def step(tile, carry):
        cols = pl.ds(pl.multiple_of(tile * 256, 256), 256)
        total_ref[:, cols] = jnp.dot(left_ref[...], table_ref[:, cols], preferred_element_type=jnp.float32)
        return carry

    lax.fori_loop(0, table_ref.shape[1] // 256, step, 0)


def square_kernel(item_count, chunk_rows, meta_ref, *refs):
    items = refs[:item_count]
    table_ref, square_ref, low_ref = refs[item_count:item_count + 3]
    store, left_store, left_ref, total_ref, sems, left_sems = refs[item_count + 3:]
    row_count = square_ref.shape[0]
    base = 0
    dest_at = 65
    left_at = 65 + item_count
    valid_at = 65 + 2 * item_count

    def copies(number):
        rows = pl.ds((number % CHUNKS) * chunk_rows, chunk_rows)
        dest = meta_ref[dest_at + number]
        left = meta_ref[left_at + number]
        main = pltpu.make_async_copy(items[number], store.at[jnp.maximum(dest, 0), rows], sems.at[number])
        side = pltpu.make_async_copy(items[number], left_store.at[jnp.maximum(left, 0), rows], left_sems.at[number])
        return dest, left, main, side

    for number in range(item_count):
        dest, left, main, side = copies(number)
        pl.when(dest >= 0)(main.start)
        pl.when(left >= 0)(side.start)
    for place in range(WINDOWS * PIECES):
        @pl.when(meta_ref[valid_at + place] == 0)
        def _():
            store[place] = jnp.zeros(store.shape[1:], store.dtype)
    for number in range(item_count):
        dest, left, main, side = copies(number)
        pl.when(dest >= 0)(main.wait)
        pl.when(left >= 0)(side.wait)

    fill_left(left_ref, lambda row: [left_store[h, row] for h in range(4)], lambda row: meta_ref[40 + row], row_count)

    def window(delta, carry):
        for row in range(row_count):
            blocks = [store[delta * PIECES + piece, row] for piece in range(PIECES)]
            at = pl.ds(pl.multiple_of(delta * 512 + row * 64, 64), 64)
            table_ref[at, :] = spread(blocks, 8 - row, 16, meta_ref[base + delta * 8 + row])
        return carry

    lax.fori_loop(0, WINDOWS, window, 0)
    product(left_ref, table_ref, total_ref)
    for row in range(row_count):
        picked = kept(total_ref[row * 64:(row + 1) * 64, :], row, meta_ref[48 + row], 512)
        square_ref[row] = picked
        low_ref[row] = picked.astype(low_ref.dtype)


def cube_kernel(meta_ref, own_ref, core_ref, x_ref, far_ref, table_ref, square_ref, out_ref, store, left_ref, total_ref):
    row_count = out_ref.shape[0]
    group = meta_ref[64]
    for bits, ref in enumerate((own_ref, core_ref, x_ref, far_ref)):
        store[group ^ bits] = ref[...]
    fill_left(left_ref, lambda row: [store[h, row] for h in range(4)], lambda row: meta_ref[56 + row], row_count)
    product(left_ref, table_ref, total_ref)
    for row in range(row_count):
        cube = kept(total_ref[row * 64:(row + 1) * 64, :], row, meta_ref[48 + row], 512)
        out_ref[row] = (3.0 * square_ref[row] - 2.0 * cube).astype(out_ref.dtype)


def missing_places(index, rows, total_rows, reach):
    places = (index - rows[:, None] + reach) % total_rows
    slots = jnp.arange(index.shape[1], dtype=jnp.int32)[None, :]
    return jnp.sum((places == slots).astype(jnp.int32), axis=1)


def per_device(dom_count, ka_count, x_blocks, col_index, prod_index):
    row_count, block, width = x_blocks.shape
    reach = 2 * row_count
    total_rows = row_count * dom_count
    dom = lax.axis_index("dom")
    group = lax.axis_index("ka")
    x_side, y_side = group // 2, dom % 2
    route = routes(dom_count, ka_count)
    steps = jnp.arange(row_count, dtype=jnp.int32)
    rows = dom * row_count + steps
    col_missing = missing_places(col_index, rows, total_rows, reach)
    prod_missing = missing_places(prod_index, rows, total_rows, reach)

    def along(value, distance):
        return lax.ppermute(value, "dom", [(d, (d - distance) % dom_count) for d in range(dom_count)])

    missing = []
    for delta in range(-2, 3):
        there = (dom + delta) % dom_count * row_count + steps
        index = col_index if delta == 0 else along(col_index, delta)
        missing.append(missing_places(index, there, total_rows, reach))

    sign = 2 * x_side - 1
    same = x_side == y_side
    chunk_rows = row_count // CHUNKS
    kinds = {}

    def add(name, chunk, array, delta, held, valid):
        kinds.setdefault(name, []).append((array, delta, held, valid))

    for chunk in range(CHUNKS):
        own = x_blocks[chunk * chunk_rows:(chunk + 1) * chunk_rows]
        za = permuted(own, route["za"])
        zb = permuted(own, route["zb"])
        ox = permuted(own, route["x"])
        oy = permuted(own, route["y"])
        do = permuted(own, route["d_other"])
        bx = permuted(za, route["x"])
        by_a = permuted(za, route["y_same"])
        by_b = permuted(zb, route["y_other"])
        da = permuted(za, route["d_same"])
        near = 1 - 2 * y_side
        far = -near
        held = (
            ("own", own, 0, group, True, "core"),
            ("za", za, -2 * sign, group, True, "core_za"),
            ("zb", zb, 2 * sign, group, True, "core_zb"),
            ("ox", ox, 0, group ^ 2, True, "core"),
            ("oy", oy, near, group, True, "core"),
            ("do", do, sign, group ^ 2, jnp.logical_not(same), "core"),
            ("bx", bx, 2 * sign, group ^ 2, True, "core"),
            ("by_a", by_a, far, group, jnp.logical_not(same), "core"),
            ("by_b", by_b, far, group, same, "core"),
            ("da", da, sign, group ^ 2, same, "core"),
        )
        for name, array, delta, shard, valid, core_route in held:
            add(name, chunk, array, delta, shard, valid)
            valid_core = valid
            if core_route == "core_za":
                valid_core = (group == 1) | (group == 2)
            if core_route == "core_zb":
                valid_core = (group == 0) | (group == 3)
            add(name + "_core", chunk, permuted(array, route[core_route]), delta, shard ^ 1, valid_core)

    items, dests, lefts = [], [], []
    for entries in kinds.values():
        for array, delta, shard, valid in entries:
            piece = shard - group + delta + 1
            dest = (delta + 2) * PIECES + piece
            dests.append(jnp.where(valid & (piece >= 0) & (piece < PIECES), dest, -1))
            lefts.append(jnp.where(valid & (jnp.asarray(delta) == 0), shard, -1))
            items.append(array)
    valid_places = []
    for delta in range(-2, 3):
        for piece in range(PIECES):
            shard = group - delta - 1 + piece
            valid_places.append(((shard >= 0) & (shard < ka_count)).astype(jnp.int32))
    table_places = [
        missing[delta + 2] - 8 * (group - delta) + steps for delta in range(-2, 3)
    ]
    meta = jnp.concatenate(
        table_places
        + [col_missing + steps, prod_missing - 8 * group, prod_missing + steps, group[None]]
        + [jnp.stack(dests), jnp.stack(lefts), jnp.stack(valid_places)]
    ).astype(jnp.int32)

    smem = pl.BlockSpec(memory_space=pltpu.SMEM)
    vmem = pl.BlockSpec(memory_space=pltpu.VMEM)
    anywhere = pl.BlockSpec(memory_space=pl.ANY)
    depth = WINDOWS * 8 * block
    table, square, low = pl.pallas_call(
        functools.partial(square_kernel, len(items), chunk_rows),
        out_shape=(
            jax.ShapeDtypeStruct((depth, 16 * block), jnp.bfloat16),
            jax.ShapeDtypeStruct((row_count, block, width), jnp.float32),
            jax.ShapeDtypeStruct((row_count, block, width), jnp.bfloat16),
        ),
        in_specs=[smem] + [anywhere] * len(items),
        out_specs=(vmem, vmem, vmem),
        scratch_shapes=[
            pltpu.VMEM((WINDOWS * PIECES, row_count, block, width), jnp.bfloat16),
            pltpu.VMEM((ka_count, row_count, block, width), jnp.bfloat16),
            pltpu.VMEM((row_count * block, depth), jnp.bfloat16),
            pltpu.VMEM((row_count * block, 16 * block), jnp.float32),
            pltpu.SemaphoreType.DMA((len(items),)),
            pltpu.SemaphoreType.DMA((len(items),)),
        ],
    )(meta, *items)
    low_core = permuted(low, route["core"])
    low_x = permuted(low, route["x"])
    low_far = permuted(low_x, route["core"])
    return pl.pallas_call(
        cube_kernel,
        out_shape=jax.ShapeDtypeStruct((row_count, block, width), jnp.bfloat16),
        in_specs=[smem] + [vmem] * 6,
        out_specs=vmem,
        scratch_shapes=[
            pltpu.VMEM((ka_count, row_count, block, width), jnp.bfloat16),
            pltpu.VMEM((row_count * block, depth), jnp.bfloat16),
            pltpu.VMEM((row_count * block, 16 * block), jnp.float32),
        ],
    )(meta, low, low_core, low_x, low_far, table, square)


def solution(mesh):
    return jax.shard_map(
        functools.partial(per_device, mesh.shape["dom"], mesh.shape["ka"]),
        mesh=mesh,
        in_specs=(P("dom", None, "ka"), P("dom", None), P("dom", None)),
        out_specs=P("dom", None, "ka"),
        check_vma=False,
    )
```

```python
import functools

import jax
import jax.numpy as jnp
from jax import lax
from jax.experimental import pallas as pl
from jax.experimental.pallas import tpu as pltpu
from jax.sharding import PartitionSpec as P

WINDOWS = 5
PIECES = 3


def permuted(value, pairs):
    return lax.ppermute(value, ("dom", "ka"), pairs)


def routes(dom_count, ka_count):
    def pairs(target):
        out = []
        for dom in range(dom_count):
            for group in range(ka_count):
                to = target(dom, group, group // 2, dom % 2)
                if to is not None:
                    out.append((dom * ka_count + group, (to[0] % dom_count) * ka_count + to[1]))
        return out

    def core(takers):
        return pairs(lambda d, g, x, y: (d, g ^ 1) if (g ^ 1) in takers(x, y) else None)

    return {
        "za": pairs(lambda d, g, x, y: (d + 2 if x else d - 2, g)),
        "zb": pairs(lambda d, g, x, y: (d - 2 if x else d + 2, g)),
        "x": pairs(lambda d, g, x, y: (d, g ^ 2)),
        "y": pairs(lambda d, g, x, y: (d ^ 1, g)),
        "dd": pairs(lambda d, g, x, y: (d + 1 if x else d - 1, g ^ 2)),
        "core": core(lambda x, y: (0, 1, 2, 3)),
        "core_dd": core(lambda x, y: (1, 2)),
        "core_oy": core(lambda x, y: ((1, 0), (3, 2))[x][y:y + 1]),
        "core_by": core(lambda x, y: ((0, 1), (2, 3))[x][y:y + 1]),
    }


def spread(pieces, shift, width, threshold):
    wide = jnp.concatenate(pieces, axis=1)
    low = wide[:, shift * 64:(shift + width) * 64]
    high = wide[:, (shift - 1) * 64:(shift - 1 + width) * 64]
    place = lax.broadcasted_iota(jnp.int32, low.shape, 1)
    zero = jnp.zeros_like(low)
    return jnp.where(place < threshold * 64, low, jnp.where(place >= threshold * 64 + 64, high, zero))


def kept(total, row, threshold, width):
    low = total[:, row * 64:row * 64 + width]
    high = total[:, (row + 1) * 64:(row + 1) * 64 + width]
    place = lax.broadcasted_iota(jnp.int32, low.shape, 1)
    return jnp.where(place < threshold * 64, low, high)


def fill_left(left_ref, rows_of, threshold, order, row_count):
    for row in range(row_count):
        blocks = rows_of(row)
        pad = jnp.zeros((64, 512), blocks[0].dtype)
        dense = spread([pad] + blocks + [pad], 8 - row, WINDOWS * 8, threshold(row))
        for window in range(WINDOWS):
            at = pl.ds(pl.multiple_of(order(window) * 512, 512), 512)
            left_ref[row * 64:(row + 1) * 64, at] = dense[:, window * 512:(window + 1) * 512]


def collect(store, items, dest, valid):
    for number, item in enumerate(items):
        @pl.when(dest(number) >= 0)
        def _():
            store[dest(number)] = item[...]
    for place in range(store.shape[0]):
        @pl.when(valid(place) == 0)
        def _():
            store[place] = jnp.zeros(store.shape[1:], store.dtype)


def near_kernel(meta_ref, dest_ref, *refs):
    items = refs[:8]
    left_ref, table_ref, total_ref, store, left_store = refs[8:]
    row_count = items[0].shape[0]
    collect(store, items, lambda n: dest_ref[n], lambda p: dest_ref[16 + p])
    for number in range(4):
        left_store[dest_ref[8 + number]] = items[number][...]
    fill_left(left_ref, lambda row: [left_store[h, row] for h in range(4)],
              lambda row: meta_ref[row], lambda chunk: meta_ref[24 + chunk], row_count)
    for window in range(2):
        for row in range(row_count):
            blocks = [store[window * PIECES + piece, row] for piece in range(PIECES)]
            at = window * 512 + row * 64
            table_ref[at:at + 64, :] = spread(blocks, 8 - row, 16, dest_ref[22 + window * 8 + row])

    def step(tile, carry):
        cols = pl.ds(pl.multiple_of(tile * 256, 256), 256)
        total_ref[:, cols] = jnp.dot(
            left_ref[:, :1024], table_ref[:, cols], preferred_element_type=jnp.float32
        )
        return carry

    lax.fori_loop(0, 4, step, 0)


def far_kernel(meta_ref, dest_ref, left_ref, before_ref, *refs):
    items = refs[:9]
    table_ref, square_ref, low_ref, store, total_ref = refs[9:]
    row_count = items[0].shape[0]
    collect(store, items, lambda n: dest_ref[n], lambda p: dest_ref[9 + p])
    for window in range(3):
        for row in range(row_count):
            blocks = [store[window * PIECES + piece, row] for piece in range(PIECES)]
            at = window * 512 + row * 64
            table_ref[at:at + 64, :] = spread(blocks, 8 - row, 16, dest_ref[18 + window * 8 + row])

    def step(tile, carry):
        cols = pl.ds(pl.multiple_of(tile * 256, 256), 256)
        total_ref[:, cols] = before_ref[:, cols] + jnp.dot(
            left_ref[:, 1024:], table_ref[:, cols], preferred_element_type=jnp.float32
        )
        return carry

    lax.fori_loop(0, 4, step, 0)
    for row in range(row_count):
        picked = kept(total_ref[row * 64:(row + 1) * 64, :], row, meta_ref[8 + row], 512)
        square_ref[row] = picked
        low_ref[row] = picked.astype(low_ref.dtype)


def cube_kernel(meta_ref, own_ref, core_ref, x_ref, far_ref, table_a, table_b, square_ref, out_ref,
                store, left_ref, total_ref):
    row_count = out_ref.shape[0]
    group = meta_ref[29]
    for bits, ref in enumerate((own_ref, core_ref, x_ref, far_ref)):
        store[group ^ bits] = ref[...]
    fill_left(left_ref, lambda row: [store[h, row] for h in range(4)],
              lambda row: meta_ref[16 + row], lambda chunk: meta_ref[24 + chunk], row_count)

    def step(tile, carry):
        cols = pl.ds(pl.multiple_of(tile * 256, 256), 256)
        total_ref[:, cols] = (
            jnp.dot(left_ref[:, :1024], table_a[:, cols], preferred_element_type=jnp.float32)
            + jnp.dot(left_ref[:, 1024:], table_b[:, cols], preferred_element_type=jnp.float32)
        )
        return carry

    lax.fori_loop(0, 4, step, 0)
    for row in range(row_count):
        cube = kept(total_ref[row * 64:(row + 1) * 64, :], row, meta_ref[8 + row], 512)
        out_ref[row] = (3.0 * square_ref[row] - 2.0 * cube).astype(out_ref.dtype)


def missing_places(index, rows, total_rows, reach):
    places = (index - rows[:, None] + reach) % total_rows
    slots = jnp.arange(index.shape[1], dtype=jnp.int32)[None, :]
    return jnp.sum((places == slots).astype(jnp.int32), axis=1)


def per_device(dom_count, ka_count, x_blocks, col_index, prod_index):
    row_count, block, width = x_blocks.shape
    reach = 2 * row_count
    total_rows = row_count * dom_count
    dom = lax.axis_index("dom")
    group = lax.axis_index("ka")
    x_side, y_side = group // 2, dom % 2
    sign = 2 * x_side - 1
    same = x_side == y_side
    other = jnp.logical_not(same)
    near = 1 - 2 * y_side
    route = routes(dom_count, ka_count)
    steps = jnp.arange(row_count, dtype=jnp.int32)

    def missing(index, delta):
        there = (dom + delta) % dom_count * row_count + steps
        return missing_places(index, there, total_rows, reach)

    def along(value, source):
        return lax.ppermute(value, "dom", [(source(d) % dom_count, d) for d in range(dom_count)])

    own = x_blocks
    za = permuted(own, route["za"])
    zb = permuted(own, route["zb"])
    ox = permuted(own, route["x"])
    oy = permuted(own, route["y"])
    dd = permuted(own, route["dd"])
    own_core = permuted(own, route["core"])
    late_index, ox = lax.optimization_barrier((col_index, ox))
    ox_core = permuted(ox, route["core"])
    oy_core = permuted(oy, route["core_oy"])
    dd_core = permuted(dd, route["core_dd"])
    bx = permuted(za, route["x"])
    by = permuted(jnp.where(same, za, zb), route["y"])
    z_core = permuted(jnp.where((group == 0) | (group == 3), za, zb), route["core"])
    bx_core = permuted(bx, route["core"])
    by_core = permuted(by, route["core_by"])

    place = {0: missing(col_index, 0)}
    place["near"] = missing(along(late_index, lambda d: d ^ 1), near)
    place["far"] = missing(along(late_index, lambda d: d + 1 if d % 2 else d - 1), -near)
    place[-2] = missing(along(late_index, lambda d: d - 2), -2)
    place[2] = missing(along(late_index, lambda d: d + 2), 2)
    prod_place = missing(prod_index, 0)

    def dest_of(entries, window_of):
        out = []
        for delta, shard, valid in entries:
            piece = shard - group + delta + 1
            ok = valid & (piece >= 0) & (piece < PIECES)
            out.append(jnp.where(ok, window_of(delta) * PIECES + piece, -1))
        return out

    def valid_of(delta):
        shards = [group - delta - 1 + piece for piece in range(PIECES)]
        return [((shard >= 0) & (shard < ka_count)).astype(jnp.int32) for shard in shards]

    def threshold(delta, key):
        return place[key] - 8 * (group - delta) + steps

    def table_of(scalars, vectors):
        return jnp.concatenate([jnp.stack(scalars)] + vectors).astype(jnp.int32)

    order = [jnp.int32(3), 2 - (near == -1), jnp.int32(0), 2 - (near == 1), jnp.int32(4)]
    meta = jnp.concatenate(
        [place[0] + steps, prod_place - 8 * group, prod_place + steps, jnp.stack(order + [group])]
    ).astype(jnp.int32)

    yes = jnp.bool_(True)
    near_items = (own, own_core, ox, ox_core, oy, oy_core, dd, dd_core)
    near_dest = dest_of(
        [(0, group ^ bits, yes) for bits in range(4)]
        + [(near, group, yes), (near, group ^ 1, yes), (near, group ^ 2, other), (near, group ^ 3, other)],
        lambda delta: 0 if isinstance(delta, int) else 1,
    )
    near_table = table_of(
        near_dest + [group ^ bits for bits in range(4)] + [group * 0] * 4 + valid_of(0) + valid_of(near),
        [threshold(0, 0), threshold(near, "near")],
    )
    far_items = (za, zb, z_core, bx, bx_core, by, by_core, dd, dd_core)
    far_dest = dest_of(
        [
            (-2 * sign, group, yes),
            (2 * sign, group, yes),
            (jnp.where((group == 0) | (group == 2), -2, 2), group ^ 1, yes),
            (2 * sign, group ^ 2, yes),
            (2 * sign, group ^ 3, yes),
            (-near, group, yes),
            (-near, group ^ 1, yes),
            (-near, group ^ 2, same),
            (-near, group ^ 3, same),
        ],
        lambda delta: jnp.where(delta == -2, 1, jnp.where(delta == 2, 2, 0)),
    )
    far_table = table_of(
        far_dest + valid_of(-near) + valid_of(-2) + valid_of(2),
        [threshold(-near, "far"), threshold(-2, -2), threshold(2, 2)],
    )

    smem = pl.BlockSpec(memory_space=pltpu.SMEM)
    vmem = pl.BlockSpec(memory_space=pltpu.VMEM)
    rows, depth, columns = row_count * block, WINDOWS * 8 * block, 16 * block
    shape = jax.ShapeDtypeStruct
    bf16, f32 = jnp.bfloat16, jnp.float32

    small = pltpu.CompilerParams(vmem_limit_bytes=28 << 20)

    def cost(k):
        return pl.CostEstimate(flops=2 * rows * k * columns * 2, bytes_accessed=12 << 20, transcendentals=0)

    left, table_a, total = pl.pallas_call(
        near_kernel,
        out_shape=(shape((rows, depth), bf16), shape((1024, columns), bf16), shape((rows, columns), f32)),
        in_specs=[smem, smem] + [vmem] * 8,
        out_specs=(vmem, vmem, vmem),
        scratch_shapes=[
            pltpu.VMEM((2 * PIECES, row_count, block, width), bf16),
            pltpu.VMEM((ka_count, row_count, block, width), bf16),
        ],
        compiler_params=small,
        cost_estimate=cost(1024),
    )(meta, near_table, *near_items)

    table_b, square, low = pl.pallas_call(
        far_kernel,
        out_shape=(
            shape((1536, columns), bf16),
            shape((row_count, block, width), f32),
            shape((row_count, block, width), bf16),
        ),
        in_specs=[smem, smem] + [vmem] * 11,
        out_specs=(vmem, vmem, vmem),
        scratch_shapes=[
            pltpu.VMEM((3 * PIECES, row_count, block, width), bf16),
            pltpu.VMEM((rows, columns), f32),
        ],
        compiler_params=small,
        cost_estimate=cost(1536),
    )(meta, far_table, left, total, *far_items)

    low_x = permuted(low, route["x"])
    low_core = permuted(low, route["core"])
    low_far = permuted(low_x, route["core"])
    return pl.pallas_call(
        cube_kernel,
        out_shape=shape((row_count, block, width), bf16),
        in_specs=[smem] + [vmem] * 7,
        out_specs=vmem,
        scratch_shapes=[
            pltpu.VMEM((ka_count, row_count, block, width), bf16),
            pltpu.VMEM((rows, depth), bf16),
            pltpu.VMEM((rows, columns), f32),
        ],
        compiler_params=small,
    )(meta, low, low_core, low_x, low_far, table_a, table_b, square)


def solution(mesh):
    return jax.shard_map(
        functools.partial(per_device, mesh.shape["dom"], mesh.shape["ka"]),
        mesh=mesh,
        in_specs=(P("dom", None, "ka"), P("dom", None), P("dom", None)),
        out_specs=P("dom", None, "ka"),
        check_vma=False,
    )
```

```python
import jax
import jax.numpy as jnp
from jax import lax
from jax.experimental import pallas as pl
from jax.experimental.pallas import tpu as pltpu
from jax.sharding import PartitionSpec as P


WINDOWS = 5
PIECES = 3


def permuted(value, pairs):
    return lax.ppermute(value, ("dom", "ka"), pairs)


def routes(dom_count, ka_count):
    def pairs(target):
        out = []
        for dom in range(dom_count):
            for group in range(ka_count):
                to = target(dom, group, group // 2, dom % 2)
                if to is not None:
                    out.append((dom * ka_count + group, (to[0] % dom_count) * ka_count + to[1]))
        return out

    def core(takers):
        return pairs(lambda d, g, x, y: (d, g ^ 1) if (g ^ 1) in takers(x, y) else None)

    return {
        "za": pairs(lambda d, g, x, y: (d + 2 if x else d - 2, g)),
        "zb": pairs(lambda d, g, x, y: (d - 2 if x else d + 2, g)),
        "x": pairs(lambda d, g, x, y: (d, g ^ 2)),
        "y": pairs(lambda d, g, x, y: (d ^ 1, g)),
        "dd": pairs(lambda d, g, x, y: (d + 1 if x else d - 1, g ^ 2)),
        "core": core(lambda x, y: (0, 1, 2, 3)),
        "core_dd": core(lambda x, y: (1, 2)),
        "core_oy": core(lambda x, y: ((1, 0), (3, 2))[x][y:y + 1]),
        "core_by": core(lambda x, y: ((0, 1), (2, 3))[x][y:y + 1]),
    }


def spread(pieces, shift, width, threshold):
    wide = jnp.concatenate(pieces, axis=1)
    low = wide[:, shift * 64:(shift + width) * 64]
    high = wide[:, (shift - 1) * 64:(shift - 1 + width) * 64]
    place = lax.broadcasted_iota(jnp.int32, low.shape, 1)
    zero = jnp.zeros_like(low)
    return jnp.where(place < threshold * 64, low, jnp.where(place >= threshold * 64 + 64, high, zero))


def kept(total, row, threshold, width):
    low = total[:, row * 64:row * 64 + width]
    high = total[:, (row + 1) * 64:(row + 1) * 64 + width]
    place = lax.broadcasted_iota(jnp.int32, low.shape, 1)
    return jnp.where(place < threshold * 64, low, high)


def fill_left(left_ref, rows_of, threshold, order, row_count):
    for row in range(row_count):
        blocks = rows_of(row)
        pad = jnp.zeros((64, 512), blocks[0].dtype)
        dense = spread([pad] + blocks + [pad], 8 - row, WINDOWS * 8, threshold(row))
        for window in range(WINDOWS):
            at = pl.ds(pl.multiple_of(order(window) * 512, 512), 512)
            left_ref[row * 64:(row + 1) * 64, at] = dense[:, window * 512:(window + 1) * 512]


def collect(store, items, dest, valid):
    for number, item in enumerate(items):
        @pl.when(dest(number) >= 0)
        def _():
            store[dest(number)] = item[...]
    for place in range(store.shape[0]):
        @pl.when(valid(place) == 0)
        def _():
            store[place] = jnp.zeros(store.shape[1:], store.dtype)


def zero_invalid(store, valid):
    for place in range(store.shape[0]):
        @pl.when(valid(place) == 0)
        def _():
            store[place] = jnp.zeros(store.shape[1:], store.dtype)


def collected(items, store, sems, dest):
    copies = []
    for number, item in enumerate(items):
        place = dest(number)
        copy = pltpu.make_async_copy(item, store.at[jnp.maximum(place, 0)], sems.at[number])
        copies.append((place >= 0, copy))
    return copies


def start_all(copies):
    for needed, copy in copies:
        pl.when(needed)(copy.start)


def wait_all(copies):
    for needed, copy in copies:
        pl.when(needed)(copy.wait)


def windows(store, table_ref, count, threshold):
    row_count = store.shape[1]
    for window in range(count):
        for row in range(row_count):
            blocks = [store[window * PIECES + piece, row] for piece in range(PIECES)]
            at = window * 512 + row * 64
            table_ref[at:at + 64, :] = spread(blocks, 8 - row, 16, threshold(window * 8 + row))


def product(left_ref, table_ref, total_ref, before_ref=None):
    depth = table_ref.shape[0]

    def step(tile, carry):
        cols = pl.ds(pl.multiple_of(tile * 256, 256), 256)
        value = jnp.dot(left_ref[:, :depth], table_ref[:, cols], preferred_element_type=jnp.float32)
        total_ref[:, cols] = value if before_ref is None else before_ref[:, cols] + value
        return carry

    lax.fori_loop(0, table_ref.shape[1] // 256, step, 0)


def near_kernel(meta_ref, dest_ref, *refs):
    items = refs[:8]
    left_out, table_out, total_out, left_store, store, left, left_far, table, total, sems, left_sems, out_sems = refs[8:]
    row_count = left_store.shape[1]
    left_in = [
        pltpu.make_async_copy(items[n], left_store.at[dest_ref[8 + n]], left_sems.at[n]) for n in range(4)
    ]
    for copy in left_in:
        copy.start()
    copies = collected(items, store, sems, lambda n: dest_ref[n])
    start_all(copies)
    zero_invalid(store, lambda p: dest_ref[16 + p])
    for copy in left_in:
        copy.wait()
    for row in range(row_count):
        pad = jnp.zeros((64, 512), left.dtype)
        blocks = [pad] + [left_store[h, row] for h in range(4)] + [pad]
        dense = spread(blocks, 8 - row, WINDOWS * 8, meta_ref[row])
        rows = slice(row * 64, (row + 1) * 64)
        left[rows, :512] = dense[:, 1024:1536]
        left_far[rows, 512:1024] = dense[:, :512]
        left_far[rows, 1024:] = dense[:, 2048:]

        @pl.when(meta_ref[30] > 0)
        def _():
            left[rows, 512:] = dense[:, 1536:2048]
            left_far[rows, :512] = dense[:, 512:1024]

        @pl.when(meta_ref[30] < 0)
        def _():
            left[rows, 512:] = dense[:, 512:1024]
            left_far[rows, :512] = dense[:, 1536:2048]
    outs = [pltpu.make_async_copy(*pair, out_sems.at[n]) for n, pair in enumerate(
        ((left_far, left_out), (table, table_out), (total, total_out)))]
    outs[0].start()
    wait_all(copies)
    windows(store, table, 2, lambda at: dest_ref[22 + at])
    outs[1].start()
    product(left, table, total)
    outs[2].start()
    for copy in outs:
        copy.wait()


def far_kernel(meta_ref, dest_ref, left_ref, before_ref, *refs):
    items = refs[:9]
    table_ref, square_ref, low_ref, store, total_ref = refs[9:]
    row_count = items[0].shape[0]
    collect(store, items, lambda n: dest_ref[n], lambda p: dest_ref[9 + p])
    for window in range(3):
        for row in range(row_count):
            blocks = [store[window * PIECES + piece, row] for piece in range(PIECES)]
            at = window * 512 + row * 64
            table_ref[at:at + 64, :] = spread(blocks, 8 - row, 16, dest_ref[18 + window * 8 + row])

    def step(tile, carry):
        cols = pl.ds(pl.multiple_of(tile * 256, 256), 256)
        total_ref[:, cols] = before_ref[:, cols] + jnp.dot(
            left_ref[...], table_ref[:, cols], preferred_element_type=jnp.float32
        )
        return carry

    lax.fori_loop(0, 4, step, 0)
    for row in range(row_count):
        picked = kept(total_ref[row * 64:(row + 1) * 64, :], row, meta_ref[8 + row], 512)
        square_ref[row] = picked
        low_ref[row] = picked.astype(low_ref.dtype)


def cube_kernel(meta_ref, own_ref, core_ref, x_ref, far_ref, table_a, table_b, square_ref, out_ref,
                store, left_ref, total_ref):
    row_count = out_ref.shape[0]
    group = meta_ref[29]
    for bits, ref in enumerate((own_ref, core_ref, x_ref, far_ref)):
        store[group ^ bits] = ref[...]
    fill_left(left_ref, lambda row: [store[h, row] for h in range(4)],
              lambda row: meta_ref[16 + row], lambda chunk: meta_ref[24 + chunk], row_count)

    def step(tile, carry):
        cols = pl.ds(pl.multiple_of(tile * 256, 256), 256)
        total_ref[:, cols] = (
            jnp.dot(left_ref[:, :1024], table_a[:, cols], preferred_element_type=jnp.float32)
            + jnp.dot(left_ref[:, 1024:], table_b[:, cols], preferred_element_type=jnp.float32)
        )
        return carry

    lax.fori_loop(0, 4, step, 0)
    for row in range(row_count):
        cube = kept(total_ref[row * 64:(row + 1) * 64, :], row, meta_ref[8 + row], 512)
        out_ref[row] = (3.0 * square_ref[row] - 2.0 * cube).astype(out_ref.dtype)


def missing_places(index, rows, total_rows, reach):
    places = (index - rows[:, None] + reach) % total_rows
    slots = jnp.arange(index.shape[1], dtype=jnp.int32)[None, :]
    return jnp.sum((places == slots).astype(jnp.int32), axis=1)


def per_device(dom_count, ka_count, x_blocks, col_index, prod_index):
    row_count, block, width = x_blocks.shape
    reach = 2 * row_count
    total_rows = row_count * dom_count
    dom = lax.axis_index("dom")
    group = lax.axis_index("ka")
    x_side, y_side = group // 2, dom % 2
    sign = 2 * x_side - 1
    same = x_side == y_side
    other = jnp.logical_not(same)
    near = 1 - 2 * y_side
    route = routes(dom_count, ka_count)
    steps = jnp.arange(row_count, dtype=jnp.int32)

    def missing(index, delta):
        there = (dom + delta) % dom_count * row_count + steps
        return missing_places(index, there, total_rows, reach)

    def along(value, source):
        return lax.ppermute(value, "dom", [(source(d) % dom_count, d) for d in range(dom_count)])

    from_near = along(col_index, lambda d: d ^ 1)
    from_far = along(col_index, lambda d: d + 1 if d % 2 else d - 1)
    from_before = along(col_index, lambda d: d - 2)
    from_after = along(col_index, lambda d: d + 2)
    own = x_blocks
    za = permuted(own, route["za"])
    zb = permuted(own, route["zb"])
    ox = permuted(own, route["x"])
    oy = permuted(own, route["y"])
    dd = permuted(own, route["dd"])
    own_core = permuted(own, route["core"])
    ox_core = permuted(ox, route["core"])
    oy_core = permuted(oy, route["core_oy"])
    dd_core = permuted(dd, route["core_dd"])
    bx = permuted(za, route["x"])
    by = permuted(jnp.where(same, za, zb), route["y"])
    z_core = permuted(jnp.where((group == 0) | (group == 3), za, zb), route["core"])
    from_near, from_far, from_before, from_after, bx = lax.optimization_barrier(
        (from_near, from_far, from_before, from_after, bx)
    )
    bx_core = permuted(bx, route["core"])
    by_core = permuted(by, route["core_by"])

    place = {0: missing(col_index, 0), "near": missing(from_near, near), "far": missing(from_far, -near),
             -2: missing(from_before, -2), 2: missing(from_after, 2)}
    prod_place = missing(prod_index, 0)

    def dest_of(entries, window_of):
        out = []
        for delta, shard, valid in entries:
            piece = shard - group + delta + 1
            ok = valid & (piece >= 0) & (piece < PIECES)
            out.append(jnp.where(ok, window_of(delta) * PIECES + piece, -1))
        return out

    def valid_of(delta):
        shards = [group - delta - 1 + piece for piece in range(PIECES)]
        return [((shard >= 0) & (shard < ka_count)).astype(jnp.int32) for shard in shards]

    def threshold(delta, key):
        return place[key] - 8 * (group - delta) + steps

    def table_of(scalars, vectors):
        return jnp.concatenate([jnp.stack(scalars)] + vectors).astype(jnp.int32)

    order = [jnp.int32(3), 2 - (near == -1), jnp.int32(0), 2 - (near == 1), jnp.int32(4)]
    meta = jnp.concatenate(
        [place[0] + steps, prod_place - 8 * group, prod_place + steps, jnp.stack(order + [group, near])]
    ).astype(jnp.int32)

    yes = jnp.bool_(True)
    near_items = (own, own_core, ox, ox_core, oy, oy_core, dd, dd_core)
    near_dest = dest_of(
        [(0, group ^ bits, yes) for bits in range(4)]
        + [(near, group, yes), (near, group ^ 1, yes), (near, group ^ 2, other), (near, group ^ 3, other)],
        lambda delta: 0 if isinstance(delta, int) else 1,
    )
    near_table = table_of(
        near_dest + [group ^ bits for bits in range(4)] + [group * 0] * 4 + valid_of(0) + valid_of(near),
        [threshold(0, 0), threshold(near, "near")],
    )
    far_items = (za, zb, z_core, bx, bx_core, by, by_core, dd, dd_core)
    far_dest = dest_of(
        [
            (-2 * sign, group, yes),
            (2 * sign, group, yes),
            (jnp.where((group == 0) | (group == 2), -2, 2), group ^ 1, yes),
            (2 * sign, group ^ 2, yes),
            (2 * sign, group ^ 3, yes),
            (-near, group, yes),
            (-near, group ^ 1, yes),
            (-near, group ^ 2, same),
            (-near, group ^ 3, same),
        ],
        lambda delta: jnp.where(delta == -2, 1, jnp.where(delta == 2, 2, 0)),
    )
    far_table = table_of(
        far_dest + valid_of(-near) + valid_of(-2) + valid_of(2),
        [threshold(-near, "far"), threshold(-2, -2), threshold(2, 2)],
    )

    smem = pl.BlockSpec(memory_space=pltpu.SMEM)
    vmem = pl.BlockSpec(memory_space=pltpu.VMEM)
    hbm = pl.BlockSpec(memory_space=pltpu.HBM)
    shards = (row_count, block, width)
    rows, depth, columns = row_count * block, WINDOWS * 8 * block, 16 * block
    shape = jax.ShapeDtypeStruct
    bf16, f32 = jnp.bfloat16, jnp.float32

    small = pltpu.CompilerParams(vmem_limit_bytes=28 << 20)

    def cost(k):
        return pl.CostEstimate(flops=2 * rows * k * columns * 2, bytes_accessed=12 << 20, transcendentals=0)

    left_far, table_a, total = pl.pallas_call(
        near_kernel,
        out_shape=(pltpu.HBM((rows, 1536), bf16), pltpu.HBM((1024, columns), bf16), pltpu.HBM((rows, columns), f32)),
        in_specs=[smem, smem] + [hbm] * 8,
        out_specs=(hbm,) * 3,
        scratch_shapes=[
            pltpu.VMEM((ka_count,) + shards, bf16),
            pltpu.VMEM((2 * PIECES,) + shards, bf16),
            pltpu.VMEM((rows, 1024), bf16),
            pltpu.VMEM((rows, 1536), bf16),
            pltpu.VMEM((1024, columns), bf16),
            pltpu.VMEM((rows, columns), f32),
            pltpu.SemaphoreType.DMA((8,)),
            pltpu.SemaphoreType.DMA((4,)),
            pltpu.SemaphoreType.DMA((3,)),
        ],
        compiler_params=small,
        cost_estimate=cost(1024),
    )(meta, near_table, *[pltpu.with_memory_space_constraint(v, pltpu.HBM) for v in near_items])

    table_b, square, low = pl.pallas_call(
        far_kernel,
        out_shape=(
            shape((1536, columns), bf16),
            shape((row_count, block, width), f32),
            shape((row_count, block, width), bf16),
        ),
        in_specs=[smem, smem] + [vmem] * 11,
        out_specs=(vmem, vmem, vmem),
        scratch_shapes=[
            pltpu.VMEM((3 * PIECES, row_count, block, width), bf16),
            pltpu.VMEM((rows, columns), f32),
        ],
        compiler_params=small,
        cost_estimate=cost(1536),
    )(meta, far_table, *[pltpu.with_memory_space_constraint(v, pltpu.HBM) for v in (left_far, total, za, zb)],
      *far_items[2:7], *[pltpu.with_memory_space_constraint(v, pltpu.HBM) for v in (dd, dd_core)])

    low_x = permuted(low, route["x"])
    low_core = permuted(low, route["core"])
    low_far = permuted(low_x, route["core"])
    return pl.pallas_call(
        cube_kernel,
        out_shape=shape((row_count, block, width), bf16),
        in_specs=[smem] + [vmem] * 7,
        out_specs=vmem,
        scratch_shapes=[
            pltpu.VMEM((ka_count, row_count, block, width), bf16),
            pltpu.VMEM((rows, depth), bf16),
            pltpu.VMEM((rows, columns), f32),
        ],
        compiler_params=small,
    )(meta, low, low_core, low_x, low_far, table_a, table_b, square)


def solution(mesh):
    def body(*args):
        return per_device(mesh.shape["dom"], mesh.shape["ka"], *args)

    return jax.shard_map(
        body,
        mesh=mesh,
        in_specs=(P("dom", None, "ka"), P("dom", None), P("dom", None)),
        out_specs=P("dom", None, "ka"),
        check_vma=False,
    )
```

```python
import jax
import jax.numpy as jnp
from jax import lax
from jax.experimental import pallas as pl
from jax.experimental.pallas import tpu as pltpu
from jax.sharding import PartitionSpec as P


WINDOWS = 5
PIECES = 3


def permuted(value, pairs):
    return lax.ppermute(value, ("dom", "ka"), pairs)


def routes(dom_count, ka_count):
    def pairs(target):
        out = []
        for dom in range(dom_count):
            for group in range(ka_count):
                to = target(dom, group, group // 2, dom % 2)
                if to is not None:
                    out.append((dom * ka_count + group, (to[0] % dom_count) * ka_count + to[1]))
        return out

    def core(takers):
        return pairs(lambda d, g, x, y: (d, g ^ 1) if (g ^ 1) in takers(x, y) else None)

    return {
        "za": pairs(lambda d, g, x, y: (d + 2 if x else d - 2, g)),
        "zb": pairs(lambda d, g, x, y: (d - 2 if x else d + 2, g) if x != y or g in (1, 2) else None),
        "x": pairs(lambda d, g, x, y: (d, g ^ 2)),
        "y": pairs(lambda d, g, x, y: (d ^ 1, g)),
        "dd": pairs(lambda d, g, x, y: (d + 1 if x else d - 1, g ^ 2)),
        "core": core(lambda x, y: (0, 1, 2, 3)),
        "core_dd": core(lambda x, y: (1, 2)),
        "core_oy": core(lambda x, y: ((1, 0), (3, 2))[x][y:y + 1]),
        "core_by": core(lambda x, y: ((0, 1), (2, 3))[x][y:y + 1]),
    }


def spread(pieces, shift, width, threshold):
    wide = jnp.concatenate(pieces, axis=1)
    low = wide[:, shift * 64:(shift + width) * 64]
    high = wide[:, (shift - 1) * 64:(shift - 1 + width) * 64]
    place = lax.broadcasted_iota(jnp.int32, low.shape, 1)
    zero = jnp.zeros_like(low)
    return jnp.where(place < threshold * 64, low, jnp.where(place >= threshold * 64 + 64, high, zero))


def kept(total, row, threshold, width):
    low = total[:, row * 64:row * 64 + width]
    high = total[:, (row + 1) * 64:(row + 1) * 64 + width]
    place = lax.broadcasted_iota(jnp.int32, low.shape, 1)
    return jnp.where(place < threshold * 64, low, high)


def fill_left(left_ref, rows_of, threshold, order, row_count):
    for row in range(row_count):
        blocks = rows_of(row)
        pad = jnp.zeros((64, 512), blocks[0].dtype)
        dense = spread([pad] + blocks + [pad], 8 - row, WINDOWS * 8, threshold(row))
        for window in range(WINDOWS):
            at = pl.ds(pl.multiple_of(order(window) * 512, 512), 512)
            left_ref[row * 64:(row + 1) * 64, at] = dense[:, window * 512:(window + 1) * 512]


def collect(store, items, dest, valid):
    for number, item in enumerate(items):
        @pl.when(dest(number) >= 0)
        def _():
            store[dest(number)] = item[...]
    for place in range(store.shape[0]):
        @pl.when(valid(place) == 0)
        def _():
            store[place] = jnp.zeros(store.shape[1:], store.dtype)


def zero_invalid(store, valid):
    for place in range(store.shape[0]):
        @pl.when(valid(place) == 0)
        def _():
            store[place] = jnp.zeros(store.shape[1:], store.dtype)


def collected(items, store, sems, dest):
    copies = []
    for number, item in enumerate(items):
        place = dest(number)
        copy = pltpu.make_async_copy(item, store.at[jnp.maximum(place, 0)], sems.at[number])
        copies.append((place >= 0, copy))
    return copies


def start_all(copies):
    for needed, copy in copies:
        pl.when(needed)(copy.start)


def wait_all(copies):
    for needed, copy in copies:
        pl.when(needed)(copy.wait)


def windows(store, table_ref, count, threshold):
    row_count = store.shape[1]
    for window in range(count):
        for row in range(row_count):
            blocks = [store[window * PIECES + piece, row] for piece in range(PIECES)]
            at = window * 512 + row * 64
            table_ref[at:at + 64, :] = spread(blocks, 8 - row, 16, threshold(window * 8 + row))


def product(left_ref, table_ref, total_ref, before_ref=None):
    depth = table_ref.shape[0]

    def step(tile, carry):
        cols = pl.ds(pl.multiple_of(tile * 256, 256), 256)
        value = jnp.dot(left_ref[:, :depth], table_ref[:, cols], preferred_element_type=jnp.float32)
        total_ref[:, cols] = value if before_ref is None else before_ref[:, cols] + value
        return carry

    lax.fori_loop(0, table_ref.shape[1] // 256, step, 0)


def transfers(pairs, sems):
    copies = [pltpu.make_async_copy(source, target, sems.at[n]) for n, (source, target) in enumerate(pairs)]
    for copy in copies:
        copy.start()
    return copies


def own_kernel(meta_ref, dest_ref, *refs):
    items = refs[:4]
    left_near_out, left_far_out, table_out, total_out = refs[4:8]
    left_store, left, left_near, left_far, store, table, total, sems, out_sems = refs[8:]
    row_count = left_store.shape[1]
    copies = transfers([(items[n], left_store.at[dest_ref[4 + n]]) for n in range(4)], sems)
    zero_invalid(store, lambda p: dest_ref[8 + p])
    for copy in copies:
        copy.wait()
    for number in range(4):
        @pl.when(dest_ref[number] >= 0)
        def _():
            store[dest_ref[number]] = left_store[dest_ref[4 + number]]
    for row in range(row_count):
        pad = jnp.zeros((64, 512), left.dtype)
        blocks = [pad] + [left_store[h, row] for h in range(4)] + [pad]
        dense = spread(blocks, 8 - row, WINDOWS * 8, meta_ref[row])
        rows = slice(row * 64, (row + 1) * 64)
        left[rows, :] = dense[:, 1024:1536]
        left_far[rows, 512:1024] = dense[:, :512]
        left_far[rows, 1024:] = dense[:, 2048:]

        @pl.when(meta_ref[30] > 0)
        def _():
            left_near[rows, :] = dense[:, 1536:2048]
            left_far[rows, :512] = dense[:, 512:1024]

        @pl.when(meta_ref[30] < 0)
        def _():
            left_near[rows, :] = dense[:, 512:1024]
            left_far[rows, :512] = dense[:, 1536:2048]
    outs = transfers([(left_near, left_near_out), (left_far, left_far_out)], out_sems)
    windows(store, table, 1, lambda at: dest_ref[11 + at])
    outs += transfers([(table, table_out)], out_sems.at[pl.ds(2, 1)])
    product(left, table, total)
    outs += transfers([(total, total_out)], out_sems.at[pl.ds(3, 1)])
    for copy in outs:
        copy.wait()


def near_kernel(meta_ref, dest_ref, left_in, before_in, *refs):
    items = refs[:4]
    table_out, base_out, store, left, before, table, total, base, sems, in_sems, out_sems = refs[4:]
    copies = collected(items, store, sems, lambda n: dest_ref[n])
    start_all(copies)
    ins = transfers([(left_in, left), (before_in, before)], in_sems)
    zero_invalid(store, lambda p: dest_ref[4 + p])
    wait_all(copies)
    windows(store, table, 1, lambda at: dest_ref[7 + at])
    outs = transfers([(table, table_out)], out_sems)
    for copy in ins:
        copy.wait()
    product(left, table, total, before)
    for row in range(base.shape[0]):
        base[row] = kept(total[row * 64:(row + 1) * 64, :], row, meta_ref[8 + row], 512)
    outs += transfers([(base, base_out)], out_sems.at[pl.ds(1, 1)])
    for copy in outs:
        copy.wait()


def far_kernel(meta_ref, dest_ref, left_ref, base_ref, *refs):
    items = refs[:9]
    table_ref, square_ref, low_ref, store, total_ref = refs[9:]
    row_count = items[0].shape[0]
    collect(store, items, lambda n: dest_ref[n], lambda p: dest_ref[9 + p])
    for window in range(3):
        for row in range(row_count):
            blocks = [store[window * PIECES + piece, row] for piece in range(PIECES)]
            at = window * 512 + row * 64
            table_ref[at:at + 64, :] = spread(blocks, 8 - row, 16, dest_ref[18 + window * 8 + row])

    def step(tile, carry):
        cols = pl.ds(pl.multiple_of(tile * 256, 256), 256)
        total_ref[:, cols] = jnp.dot(
            left_ref[...], table_ref[:, cols], preferred_element_type=jnp.float32
        )
        return carry

    lax.fori_loop(0, 4, step, 0)
    for row in range(row_count):
        picked = base_ref[row] + kept(total_ref[row * 64:(row + 1) * 64, :], row, meta_ref[8 + row], 512)
        square_ref[row] = picked
        low_ref[row] = picked.astype(low_ref.dtype)


def cube_kernel(meta_ref, own_ref, core_ref, x_ref, far_ref, table_own, table_near, table_b, square_ref, out_ref,
                store, left_ref, total_ref):
    row_count = out_ref.shape[0]
    group = meta_ref[29]
    for bits, ref in enumerate((own_ref, core_ref, x_ref, far_ref)):
        store[group ^ bits] = ref[...]
    fill_left(left_ref, lambda row: [store[h, row] for h in range(4)],
              lambda row: meta_ref[16 + row], lambda chunk: meta_ref[24 + chunk], row_count)

    def step(tile, carry):
        cols = pl.ds(pl.multiple_of(tile * 256, 256), 256)
        total_ref[:, cols] = (
            jnp.dot(left_ref[:, :512], table_own[:, cols], preferred_element_type=jnp.float32)
            + jnp.dot(left_ref[:, 512:1024], table_near[:, cols], preferred_element_type=jnp.float32)
            + jnp.dot(left_ref[:, 1024:], table_b[:, cols], preferred_element_type=jnp.float32)
        )
        return carry

    lax.fori_loop(0, 4, step, 0)
    for row in range(row_count):
        cube = kept(total_ref[row * 64:(row + 1) * 64, :], row, meta_ref[8 + row], 512)
        out_ref[row] = (3.0 * square_ref[row] - 2.0 * cube).astype(out_ref.dtype)


def missing_places(index, rows, total_rows, reach):
    places = (index - rows[:, None] + reach) % total_rows
    slots = jnp.arange(index.shape[1], dtype=jnp.int32)[None, :]
    return jnp.sum((places == slots).astype(jnp.int32), axis=1)


def per_device(dom_count, ka_count, x_blocks, col_index, prod_index):
    row_count, block, width = x_blocks.shape
    reach = 2 * row_count
    total_rows = row_count * dom_count
    dom = lax.axis_index("dom")
    group = lax.axis_index("ka")
    x_side, y_side = group // 2, dom % 2
    sign = 2 * x_side - 1
    same = x_side == y_side
    other = jnp.logical_not(same)
    near = 1 - 2 * y_side
    route = routes(dom_count, ka_count)
    steps = jnp.arange(row_count, dtype=jnp.int32)

    def missing(index, delta):
        there = (dom + delta) % dom_count * row_count + steps
        return missing_places(index, there, total_rows, reach)

    def along(value, source):
        return lax.ppermute(value, "dom", [(source(d) % dom_count, d) for d in range(dom_count)])

    from_near = along(col_index, lambda d: d ^ 1)
    from_far = along(col_index, lambda d: d + 1 if d % 2 else d - 1)
    from_before = along(col_index, lambda d: d - 2)
    from_after = along(col_index, lambda d: d + 2)
    own = x_blocks
    za = permuted(own, route["za"])
    zb = permuted(own, route["zb"])
    ox = permuted(own, route["x"])
    oy = permuted(own, route["y"])
    dd = permuted(own, route["dd"])
    own_core = permuted(own, route["core"])
    ox_core = permuted(ox, route["core"])
    oy_core = permuted(oy, route["core_oy"])
    from_near, dd = lax.optimization_barrier((from_near, dd))
    dd_core = permuted(dd, route["core_dd"])
    bx = permuted(za, route["x"])
    by_source = jnp.where(same, za, zb)
    z_source = jnp.where((group == 0) | (group == 3), za, zb)
    by = permuted(by_source, route["y"])
    z_core = permuted(z_source, route["core"])
    from_far, from_before, from_after, bx = lax.optimization_barrier((from_far, from_before, from_after, bx))
    bx_core = permuted(bx, route["core"])
    by_core = permuted(by, route["core_by"])

    place = {0: missing(col_index, 0), "near": missing(from_near, near), "far": missing(from_far, -near),
             -2: missing(from_before, -2), 2: missing(from_after, 2)}
    prod_place = missing(prod_index, 0)

    def dest_of(entries, window_of):
        out = []
        for delta, shard, valid in entries:
            piece = shard - group + delta + 1
            ok = valid & (piece >= 0) & (piece < PIECES)
            out.append(jnp.where(ok, window_of(delta) * PIECES + piece, -1))
        return out

    def valid_of(delta):
        shards = [group - delta - 1 + piece for piece in range(PIECES)]
        return [((shard >= 0) & (shard < ka_count)).astype(jnp.int32) for shard in shards]

    def threshold(delta, key):
        return place[key] - 8 * (group - delta) + steps

    def table_of(scalars, vectors):
        return jnp.concatenate([jnp.stack(scalars)] + vectors).astype(jnp.int32)

    order = [jnp.int32(3), 2 - (near == -1), jnp.int32(0), 2 - (near == 1), jnp.int32(4)]
    meta = jnp.concatenate(
        [place[0] + steps, prod_place - 8 * group, prod_place + steps, jnp.stack(order + [group, near])]
    ).astype(jnp.int32)

    yes = jnp.bool_(True)
    own_items = (own, own_core, ox, ox_core)
    own_table = table_of(
        dest_of([(0, group ^ bits, yes) for bits in range(4)], lambda delta: 0)
        + [group ^ bits for bits in range(4)] + valid_of(0),
        [threshold(0, 0)],
    )
    near_items = (oy, oy_core, dd, dd_core)
    near_table = table_of(
        dest_of(
            [(near, group, yes), (near, group ^ 1, yes), (near, group ^ 2, other), (near, group ^ 3, other)],
            lambda delta: 0,
        )
        + valid_of(near),
        [threshold(near, "near")],
    )
    far_items = (za, zb, z_core, bx, bx_core, by, by_core, dd, dd_core)
    far_dest = dest_of(
        [
            (-2 * sign, group, yes),
            (2 * sign, group, yes),
            (jnp.where((group == 0) | (group == 2), -2, 2), group ^ 1, yes),
            (2 * sign, group ^ 2, yes),
            (2 * sign, group ^ 3, yes),
            (-near, group, yes),
            (-near, group ^ 1, yes),
            (-near, group ^ 2, same),
            (-near, group ^ 3, same),
        ],
        lambda delta: jnp.where(delta == -2, 1, jnp.where(delta == 2, 2, 0)),
    )
    far_table = table_of(
        far_dest + valid_of(-near) + valid_of(-2) + valid_of(2),
        [threshold(-near, "far"), threshold(-2, -2), threshold(2, 2)],
    )

    smem = pl.BlockSpec(memory_space=pltpu.SMEM)
    vmem = pl.BlockSpec(memory_space=pltpu.VMEM)
    hbm = pl.BlockSpec(memory_space=pltpu.HBM)
    shards = (row_count, block, width)
    rows, depth, columns = row_count * block, WINDOWS * 8 * block, 16 * block
    shape = jax.ShapeDtypeStruct
    bf16, f32 = jnp.bfloat16, jnp.float32

    small = pltpu.CompilerParams(vmem_limit_bytes=28 << 20)

    def cost(k):
        return pl.CostEstimate(flops=2 * rows * k * columns * 2, bytes_accessed=12 << 20, transcendentals=0)

    def in_hbm(*values):
        return [pltpu.with_memory_space_constraint(value, pltpu.HBM) for value in values]

    dma = pltpu.SemaphoreType.DMA
    left_near, left_far, table_own, total = pl.pallas_call(
        own_kernel,
        out_shape=(
            pltpu.HBM((rows, 512), bf16),
            pltpu.HBM((rows, 1536), bf16),
            pltpu.HBM((512, columns), bf16),
            pltpu.HBM((rows, columns), f32),
        ),
        in_specs=[smem, smem] + [hbm] * 4,
        out_specs=(hbm,) * 4,
        scratch_shapes=[
            pltpu.VMEM((ka_count,) + shards, bf16),
            pltpu.VMEM((rows, 512), bf16),
            pltpu.VMEM((rows, 512), bf16),
            pltpu.VMEM((rows, 1536), bf16),
            pltpu.VMEM((PIECES,) + shards, bf16),
            pltpu.VMEM((512, columns), bf16),
            pltpu.VMEM((rows, columns), f32),
            dma((4,)),
            dma((4,)),
        ],
        compiler_params=small,
        cost_estimate=cost(512),
    )(meta, own_table, *in_hbm(*own_items))

    table_near, base = pl.pallas_call(
        near_kernel,
        out_shape=(pltpu.HBM((512, columns), bf16), pltpu.HBM(shards, f32)),
        in_specs=[smem, smem] + [hbm] * 6,
        out_specs=(hbm, hbm),
        scratch_shapes=[
            pltpu.VMEM((PIECES,) + shards, bf16),
            pltpu.VMEM((rows, 512), bf16),
            pltpu.VMEM((rows, columns), f32),
            pltpu.VMEM((512, columns), bf16),
            pltpu.VMEM((rows, columns), f32),
            pltpu.VMEM(shards, f32),
            dma((4,)),
            dma((2,)),
            dma((2,)),
        ],
        compiler_params=small,
        cost_estimate=cost(512),
    )(meta, near_table, *in_hbm(left_near, total, *near_items))

    table_b, square, low = pl.pallas_call(
        far_kernel,
        out_shape=(
            shape((1536, columns), bf16),
            shape((row_count, block, width), f32),
            shape((row_count, block, width), bf16),
        ),
        in_specs=[smem, smem] + [vmem] * 11,
        out_specs=(vmem, vmem, vmem),
        scratch_shapes=[
            pltpu.VMEM((3 * PIECES, row_count, block, width), bf16),
            pltpu.VMEM((rows, columns), f32),
        ],
        compiler_params=small,
        cost_estimate=cost(1536),
    )(meta, far_table, *[pltpu.with_memory_space_constraint(v, pltpu.HBM) for v in (left_far, base, za, zb)],
      *far_items[2:7], *[pltpu.with_memory_space_constraint(v, pltpu.HBM) for v in (dd, dd_core)])

    low_x = permuted(low, route["x"])
    low_core = permuted(low, route["core"])
    low_far = permuted(low_x, route["core"])
    return pl.pallas_call(
        cube_kernel,
        out_shape=shape((row_count, block, width), bf16),
        in_specs=[smem] + [vmem] * 8,
        out_specs=vmem,
        scratch_shapes=[
            pltpu.VMEM((ka_count, row_count, block, width), bf16),
            pltpu.VMEM((rows, depth), bf16),
            pltpu.VMEM((rows, columns), f32),
        ],
        compiler_params=small,
    )(meta, low, low_core, low_x, low_far, table_own, table_near, table_b, square)


def solution(mesh):
    def body(*args):
        return per_device(mesh.shape["dom"], mesh.shape["ka"], *args)

    return jax.shard_map(
        body,
        mesh=mesh,
        in_specs=(P("dom", None, "ka"), P("dom", None), P("dom", None)),
        out_specs=P("dom", None, "ka"),
        check_vma=False,
    )
```

```python
import functools

import jax
import jax.numpy as jnp
from jax import lax
from jax.experimental import pallas as pl
from jax.experimental.pallas import tpu as pltpu
from jax.sharding import PartitionSpec as P


WINDOWS = 5
PIECES = 3


def permuted(value, pairs):
    return lax.ppermute(value, ("dom", "ka"), pairs)


def routes(dom_count, ka_count):
    def pairs(target):
        out = []
        for dom in range(dom_count):
            for group in range(ka_count):
                to = target(dom, group, group // 2, dom % 2)
                if to is not None:
                    out.append((dom * ka_count + group, (to[0] % dom_count) * ka_count + to[1]))
        return out

    def core(takers):
        return pairs(lambda d, g, x, y: (d, g ^ 1) if (g ^ 1) in takers(x, y) else None)

    return {
        "za": pairs(lambda d, g, x, y: (d + 2 if x else d - 2, g)),
        "zb": pairs(lambda d, g, x, y: (d - 2 if x else d + 2, g) if x != y or g in (1, 2) else None),
        "x": pairs(lambda d, g, x, y: (d, g ^ 2)),
        "y": pairs(lambda d, g, x, y: (d ^ 1, g)),
        "dd": pairs(lambda d, g, x, y: (d + 1 if x else d - 1, g ^ 2)),
        "core": core(lambda x, y: (0, 1, 2, 3)),
        "core_dd": core(lambda x, y: (1, 2)),
        "core_oy": core(lambda x, y: ((1, 0), (3, 2))[x][y:y + 1]),
        "core_by": core(lambda x, y: ((0, 1), (2, 3))[x][y:y + 1]),
    }


def spread(pieces, shift, width, threshold):
    wide = jnp.concatenate(pieces, axis=1)
    low = wide[:, shift * 64:(shift + width) * 64]
    high = wide[:, (shift - 1) * 64:(shift - 1 + width) * 64]
    place = lax.broadcasted_iota(jnp.int32, low.shape, 1)
    zero = jnp.zeros_like(low)
    return jnp.where(place < threshold * 64, low, jnp.where(place >= threshold * 64 + 64, high, zero))


def kept(total, row, threshold, width):
    low = total[:, row * 64:row * 64 + width]
    high = total[:, (row + 1) * 64:(row + 1) * 64 + width]
    place = lax.broadcasted_iota(jnp.int32, low.shape, 1)
    return jnp.where(place < threshold * 64, low, high)


def fill_left(left_ref, store, first_row, threshold, order):
    for row in range(store.shape[1]):
        pad = jnp.zeros((64, 512), store.dtype)
        blocks = [pad] + [store[h, row] for h in range(store.shape[0])] + [pad]
        dense = spread(blocks, 8 - first_row - row, WINDOWS * 8, threshold(first_row + row))
        for window in range(WINDOWS):
            at = pl.ds(pl.multiple_of(order(window) * 512, 512), 512)
            left_ref[row * 64:(row + 1) * 64, at] = dense[:, window * 512:(window + 1) * 512]


def collect(store, items, dest, valid):
    for number, item in enumerate(items):
        @pl.when(dest(number) >= 0)
        def _():
            store[dest(number)] = item[...]
    for place in range(store.shape[0]):
        @pl.when(valid(place) == 0)
        def _():
            store[place] = jnp.zeros(store.shape[1:], store.dtype)


def zero_invalid(store, valid):
    for place in range(store.shape[0]):
        @pl.when(valid(place) == 0)
        def _():
            store[place] = jnp.zeros(store.shape[1:], store.dtype)


def collected(items, store, sems, dest):
    copies = []
    for number, item in enumerate(items):
        place = dest(number)
        copy = pltpu.make_async_copy(item, store.at[jnp.maximum(place, 0)], sems.at[number])
        copies.append((place >= 0, copy))
    return copies


def start_all(copies):
    for needed, copy in copies:
        pl.when(needed)(copy.start)


def wait_all(copies):
    for needed, copy in copies:
        pl.when(needed)(copy.wait)


def windows(store, table_ref, count, threshold):
    row_count = store.shape[1]
    for window in range(count):
        for row in range(row_count):
            blocks = [store[window * PIECES + piece, row] for piece in range(PIECES)]
            at = window * 512 + row * 64
            table_ref[at:at + 64, :] = spread(blocks, 8 - row, 16, threshold(window * 8 + row))


def product(left_ref, table_ref, total_ref, before_ref=None):
    depth = table_ref.shape[0]

    def step(tile, carry):
        cols = pl.ds(pl.multiple_of(tile * 256, 256), 256)
        value = jnp.dot(left_ref[:, :depth], table_ref[:, cols], preferred_element_type=jnp.float32)
        total_ref[:, cols] = value if before_ref is None else before_ref[:, cols] + value
        return carry

    lax.fori_loop(0, table_ref.shape[1] // 256, step, 0)


def transfers(pairs, sems):
    copies = [pltpu.make_async_copy(source, target, sems.at[n]) for n, (source, target) in enumerate(pairs)]
    for copy in copies:
        copy.start()
    return copies


def own_kernel(meta_ref, dest_ref, *refs):
    items = refs[:4]
    left_near_out, left_far_out, table_out, total_out = refs[4:8]
    left_store, left, left_near, left_far, store, table, total, sems, out_sems = refs[8:]
    row_count = left_store.shape[1]
    copies = transfers([(items[n], left_store.at[dest_ref[4 + n]]) for n in range(4)], sems)
    zero_invalid(store, lambda p: dest_ref[8 + p])
    for copy in copies:
        copy.wait()
    for number in range(4):
        @pl.when(dest_ref[number] >= 0)
        def _():
            store[dest_ref[number]] = left_store[dest_ref[4 + number]]
    for row in range(row_count):
        pad = jnp.zeros((64, 512), left.dtype)
        blocks = [pad] + [left_store[h, row] for h in range(4)] + [pad]
        dense = spread(blocks, 8 - row, WINDOWS * 8, meta_ref[row])
        rows = slice(row * 64, (row + 1) * 64)
        left[rows, :] = dense[:, 1024:1536]
        left_far[rows, 512:1024] = dense[:, :512]
        left_far[rows, 1024:] = dense[:, 2048:]

        @pl.when(meta_ref[30] > 0)
        def _():
            left_near[rows, :] = dense[:, 1536:2048]
            left_far[rows, :512] = dense[:, 512:1024]

        @pl.when(meta_ref[30] < 0)
        def _():
            left_near[rows, :] = dense[:, 512:1024]
            left_far[rows, :512] = dense[:, 1536:2048]
    outs = transfers([(left_near, left_near_out), (left_far, left_far_out)], out_sems)
    windows(store, table, 1, lambda at: dest_ref[11 + at])
    outs += transfers([(table, table_out)], out_sems.at[pl.ds(2, 1)])
    product(left, table, total)
    outs += transfers([(total, total_out)], out_sems.at[pl.ds(3, 1)])
    for copy in outs:
        copy.wait()


def near_kernel(meta_ref, dest_ref, left_in, before_in, *refs):
    items = refs[:4]
    table_out, base_out, store, left, before, table, total, base, sems, in_sems, out_sems = refs[4:]
    copies = collected(items, store, sems, lambda n: dest_ref[n])
    start_all(copies)
    ins = transfers([(left_in, left), (before_in, before)], in_sems)
    zero_invalid(store, lambda p: dest_ref[4 + p])
    wait_all(copies)
    windows(store, table, 1, lambda at: dest_ref[7 + at])
    outs = transfers([(table, table_out)], out_sems)
    for copy in ins:
        copy.wait()
    product(left, table, total, before)
    for row in range(base.shape[0]):
        base[row] = kept(total[row * 64:(row + 1) * 64, :], row, meta_ref[8 + row], 512)
    outs += transfers([(base, base_out)], out_sems.at[pl.ds(1, 1)])
    for copy in outs:
        copy.wait()


def far_kernel(meta_ref, dest_ref, left_ref, base_ref, *refs):
    items = refs[:9]
    table_ref, square_ref, low_a, low_b, store, total_ref = refs[9:]
    row_count = items[0].shape[0]
    half = row_count // 2
    collect(store, items, lambda n: dest_ref[n], lambda p: dest_ref[9 + p])
    for window in range(3):
        for row in range(row_count):
            blocks = [store[window * PIECES + piece, row] for piece in range(PIECES)]
            at = window * 512 + row * 64
            table_ref[at:at + 64, :] = spread(blocks, 8 - row, 16, dest_ref[18 + window * 8 + row])

    def step(tile, carry):
        cols = pl.ds(pl.multiple_of(tile * 256, 256), 256)
        total_ref[:, cols] = jnp.dot(
            left_ref[...], table_ref[:, cols], preferred_element_type=jnp.float32
        )
        return carry

    lax.fori_loop(0, 4, step, 0)
    for row in range(row_count):
        picked = base_ref[row] + kept(total_ref[row * 64:(row + 1) * 64, :], row, meta_ref[8 + row], 512)
        square_ref[row] = picked
        low_ref = low_a if row < half else low_b
        low_ref[row % half] = picked.astype(low_ref.dtype)


def cube_kernel(part, meta_ref, own_ref, core_ref, x_ref, far_ref, table_own, table_near, table_b, square_ref, *refs):
    out_ref, store, left_ref, total_ref, result, sem = refs[part:]
    row_count = result.shape[0]
    first_row = part * row_count
    group = meta_ref[29]
    for bits, ref in enumerate((own_ref, core_ref, x_ref, far_ref)):
        store[group ^ bits] = ref[...]
    fill_left(left_ref, store, first_row, lambda row: meta_ref[16 + row], lambda window: meta_ref[24 + window])

    def step(tile, carry):
        cols = pl.ds(pl.multiple_of(tile * 256, 256), 256)
        total_ref[:, cols] = (
            jnp.dot(left_ref[:, :512], table_own[:, cols], preferred_element_type=jnp.float32)
            + jnp.dot(left_ref[:, 512:1024], table_near[:, cols], preferred_element_type=jnp.float32)
            + jnp.dot(left_ref[:, 1024:], table_b[:, cols], preferred_element_type=jnp.float32)
        )
        return carry

    lax.fori_loop(0, 4, step, 0)
    for row in range(row_count):
        whole = first_row + row
        cube = kept(total_ref[row * 64:(row + 1) * 64, :], whole, meta_ref[8 + whole], 512)
        result[row] = (3.0 * square_ref[whole] - 2.0 * cube).astype(result.dtype)
    copy = pltpu.make_async_copy(result, out_ref.at[pl.ds(first_row, row_count)], sem)
    copy.start()
    copy.wait()


def missing_places(index, rows, total_rows, reach):
    places = (index - rows[:, None] + reach) % total_rows
    slots = jnp.arange(index.shape[1], dtype=jnp.int32)[None, :]
    return jnp.sum((places == slots).astype(jnp.int32), axis=1)


def per_device(dom_count, ka_count, x_blocks, col_index, prod_index):
    row_count, block, width = x_blocks.shape
    reach = 2 * row_count
    total_rows = row_count * dom_count
    dom = lax.axis_index("dom")
    group = lax.axis_index("ka")
    x_side, y_side = group // 2, dom % 2
    sign = 2 * x_side - 1
    same = x_side == y_side
    other = jnp.logical_not(same)
    near = 1 - 2 * y_side
    route = routes(dom_count, ka_count)
    steps = jnp.arange(row_count, dtype=jnp.int32)

    def missing(index, delta):
        there = (dom + delta) % dom_count * row_count + steps
        return missing_places(index, there, total_rows, reach)

    def along(value, source):
        return lax.ppermute(value, "dom", [(source(d) % dom_count, d) for d in range(dom_count)])

    from_near = along(col_index, lambda d: d ^ 1)
    from_far = along(col_index, lambda d: d + 1 if d % 2 else d - 1)
    from_before = along(col_index, lambda d: d - 2)
    from_after = along(col_index, lambda d: d + 2)
    own = x_blocks
    za = permuted(own, route["za"])
    zb = permuted(own, route["zb"])
    ox = permuted(own, route["x"])
    oy = permuted(own, route["y"])
    dd = permuted(own, route["dd"])
    own_core = permuted(own, route["core"])
    ox_core = permuted(ox, route["core"])
    oy_core = permuted(oy, route["core_oy"])
    from_near, dd = lax.optimization_barrier((from_near, dd))
    dd_core = permuted(dd, route["core_dd"])
    bx = permuted(za, route["x"])
    by_source = jnp.where(same, za, zb)
    z_source = jnp.where((group == 0) | (group == 3), za, zb)
    by = permuted(by_source, route["y"])
    z_core = permuted(z_source, route["core"])
    from_far, from_before, from_after, bx = lax.optimization_barrier((from_far, from_before, from_after, bx))
    bx_core = permuted(bx, route["core"])
    by_core = permuted(by, route["core_by"])

    place = {0: missing(col_index, 0), "near": missing(from_near, near), "far": missing(from_far, -near),
             -2: missing(from_before, -2), 2: missing(from_after, 2)}
    prod_place = missing(prod_index, 0)

    def dest_of(entries, window_of):
        out = []
        for delta, shard, valid in entries:
            piece = shard - group + delta + 1
            ok = valid & (piece >= 0) & (piece < PIECES)
            out.append(jnp.where(ok, window_of(delta) * PIECES + piece, -1))
        return out

    def valid_of(delta):
        shards = [group - delta - 1 + piece for piece in range(PIECES)]
        return [((shard >= 0) & (shard < ka_count)).astype(jnp.int32) for shard in shards]

    def threshold(delta, key):
        return place[key] - 8 * (group - delta) + steps

    def table_of(scalars, vectors):
        return jnp.concatenate([jnp.stack(scalars)] + vectors).astype(jnp.int32)

    order = [jnp.int32(3), 2 - (near == -1), jnp.int32(0), 2 - (near == 1), jnp.int32(4)]
    meta = jnp.concatenate(
        [place[0] + steps, prod_place - 8 * group, prod_place + steps, jnp.stack(order + [group, near])]
    ).astype(jnp.int32)

    yes = jnp.bool_(True)
    own_items = (own, own_core, ox, ox_core)
    own_table = table_of(
        dest_of([(0, group ^ bits, yes) for bits in range(4)], lambda delta: 0)
        + [group ^ bits for bits in range(4)] + valid_of(0),
        [threshold(0, 0)],
    )
    near_items = (oy, oy_core, dd, dd_core)
    near_table = table_of(
        dest_of(
            [(near, group, yes), (near, group ^ 1, yes), (near, group ^ 2, other), (near, group ^ 3, other)],
            lambda delta: 0,
        )
        + valid_of(near),
        [threshold(near, "near")],
    )
    far_items = (za, zb, z_core, bx, bx_core, by, by_core, dd, dd_core)
    far_dest = dest_of(
        [
            (-2 * sign, group, yes),
            (2 * sign, group, yes),
            (jnp.where((group == 0) | (group == 2), -2, 2), group ^ 1, yes),
            (2 * sign, group ^ 2, yes),
            (2 * sign, group ^ 3, yes),
            (-near, group, yes),
            (-near, group ^ 1, yes),
            (-near, group ^ 2, same),
            (-near, group ^ 3, same),
        ],
        lambda delta: jnp.where(delta == -2, 1, jnp.where(delta == 2, 2, 0)),
    )
    far_table = table_of(
        far_dest + valid_of(-near) + valid_of(-2) + valid_of(2),
        [threshold(-near, "far"), threshold(-2, -2), threshold(2, 2)],
    )

    smem = pl.BlockSpec(memory_space=pltpu.SMEM)
    vmem = pl.BlockSpec(memory_space=pltpu.VMEM)
    hbm = pl.BlockSpec(memory_space=pltpu.HBM)
    shards = (row_count, block, width)
    rows, depth, columns = row_count * block, WINDOWS * 8 * block, 16 * block
    shape = jax.ShapeDtypeStruct
    bf16, f32 = jnp.bfloat16, jnp.float32

    small = pltpu.CompilerParams(vmem_limit_bytes=28 << 20)

    def cost(k):
        return pl.CostEstimate(flops=2 * rows * k * columns * 2, bytes_accessed=12 << 20, transcendentals=0)

    def in_hbm(*values):
        return [pltpu.with_memory_space_constraint(value, pltpu.HBM) for value in values]

    dma = pltpu.SemaphoreType.DMA
    left_near, left_far, table_own, total = pl.pallas_call(
        own_kernel,
        out_shape=(
            pltpu.HBM((rows, 512), bf16),
            pltpu.HBM((rows, 1536), bf16),
            pltpu.HBM((512, columns), bf16),
            pltpu.HBM((rows, columns), f32),
        ),
        in_specs=[smem, smem] + [hbm] * 4,
        out_specs=(hbm,) * 4,
        scratch_shapes=[
            pltpu.VMEM((ka_count,) + shards, bf16),
            pltpu.VMEM((rows, 512), bf16),
            pltpu.VMEM((rows, 512), bf16),
            pltpu.VMEM((rows, 1536), bf16),
            pltpu.VMEM((PIECES,) + shards, bf16),
            pltpu.VMEM((512, columns), bf16),
            pltpu.VMEM((rows, columns), f32),
            dma((4,)),
            dma((4,)),
        ],
        compiler_params=small,
        cost_estimate=cost(512),
    )(meta, own_table, *in_hbm(*own_items))

    table_near, base = pl.pallas_call(
        near_kernel,
        out_shape=(pltpu.HBM((512, columns), bf16), pltpu.HBM(shards, f32)),
        in_specs=[smem, smem] + [hbm] * 6,
        out_specs=(hbm, hbm),
        scratch_shapes=[
            pltpu.VMEM((PIECES,) + shards, bf16),
            pltpu.VMEM((rows, 512), bf16),
            pltpu.VMEM((rows, columns), f32),
            pltpu.VMEM((512, columns), bf16),
            pltpu.VMEM((rows, columns), f32),
            pltpu.VMEM(shards, f32),
            dma((4,)),
            dma((2,)),
            dma((2,)),
        ],
        compiler_params=small,
        cost_estimate=cost(512),
    )(meta, near_table, *in_hbm(left_near, total, *near_items))

    half_rows = row_count // 2
    table_b, square, low_a, low_b = pl.pallas_call(
        far_kernel,
        out_shape=(
            shape((1536, columns), bf16),
            shape((row_count, block, width), f32),
            shape((half_rows, block, width), bf16),
            shape((half_rows, block, width), bf16),
        ),
        in_specs=[smem, smem] + [vmem] * 11,
        out_specs=(vmem, vmem, vmem, vmem),
        scratch_shapes=[
            pltpu.VMEM((3 * PIECES, row_count, block, width), bf16),
            pltpu.VMEM((rows, columns), f32),
        ],
        compiler_params=small,
        cost_estimate=cost(1536),
    )(meta, far_table, *[pltpu.with_memory_space_constraint(v, pltpu.HBM) for v in (left_far, base, za, zb)],
      *far_items[2:7], *[pltpu.with_memory_space_constraint(v, pltpu.HBM) for v in (dd, dd_core)])

    lows = (low_a, low_b)
    by_x = [permuted(low, route["x"]) for low in lows]
    by_partner = [permuted(low, route["core"]) for low in lows]
    by_both = [permuted(low, route["core"]) for low in by_x]
    out = ()
    for part in range(2):
        out = (pl.pallas_call(
            functools.partial(cube_kernel, part),
            out_shape=pltpu.HBM((row_count, block, width), bf16),
            in_specs=[smem] + [vmem] * 8 + [hbm] * part,
            out_specs=hbm,
            scratch_shapes=[
                pltpu.VMEM((ka_count, half_rows, block, width), bf16),
                pltpu.VMEM((rows // 2, depth), bf16),
                pltpu.VMEM((rows // 2, columns), f32),
                pltpu.VMEM((half_rows, block, width), bf16),
                pltpu.SemaphoreType.DMA,
            ],
            input_output_aliases={9: 0} if part else {},
            compiler_params=small,
            cost_estimate=cost(1280),
        )(meta, lows[part], by_partner[part], by_x[part], by_both[part],
          table_own, table_near, table_b, square, *out),)
    return out[0]


def solution(mesh):
    def body(*args):
        return per_device(mesh.shape["dom"], mesh.shape["ka"], *args)

    return jax.shard_map(
        body,
        mesh=mesh,
        in_specs=(P("dom", None, "ka"), P("dom", None), P("dom", None)),
        out_specs=P("dom", None, "ka"),
        check_vma=False,
    )
```

```python
import functools

import jax
import jax.numpy as jnp
from jax import lax
from jax.experimental import pallas as pl
from jax.experimental.pallas import tpu as pltpu
from jax.sharding import PartitionSpec as P


WINDOWS = 5
PIECES = 3


def permuted(value, pairs):
    return lax.ppermute(value, ("dom", "ka"), pairs)


def routes(dom_count, ka_count):
    def pairs(target):
        out = []
        for dom in range(dom_count):
            for group in range(ka_count):
                to = target(dom, group, group // 2, dom % 2)
                if to is not None:
                    out.append((dom * ka_count + group, (to[0] % dom_count) * ka_count + to[1]))
        return out

    def core(takers):
        return pairs(lambda d, g, x, y: (d, g ^ 1) if (g ^ 1) in takers(x, y) else None)

    return {
        "za": pairs(lambda d, g, x, y: (d + 2 if x else d - 2, g)),
        "zb": pairs(lambda d, g, x, y: (d - 2 if x else d + 2, g) if x != y or g in (1, 2) else None),
        "x": pairs(lambda d, g, x, y: (d, g ^ 2)),
        "y": pairs(lambda d, g, x, y: (d ^ 1, g)),
        "dd": pairs(lambda d, g, x, y: (d + 1 if x else d - 1, g ^ 2)),
        "core": core(lambda x, y: (0, 1, 2, 3)),
        "core_dd": core(lambda x, y: (1, 2)),
        "core_oy": core(lambda x, y: ((1, 0), (3, 2))[x][y:y + 1]),
        "core_by": core(lambda x, y: ((0, 1), (2, 3))[x][y:y + 1]),
    }


def spread(pieces, shift, width, threshold):
    wide = jnp.concatenate(pieces, axis=1)
    low = wide[:, shift * 64:(shift + width) * 64]
    high = wide[:, (shift - 1) * 64:(shift - 1 + width) * 64]
    place = lax.broadcasted_iota(jnp.int32, low.shape, 1)
    zero = jnp.zeros_like(low)
    return jnp.where(place < threshold * 64, low, jnp.where(place >= threshold * 64 + 64, high, zero))


def kept(total, row, threshold, width):
    low = total[:, row * 64:row * 64 + width]
    high = total[:, (row + 1) * 64:(row + 1) * 64 + width]
    place = lax.broadcasted_iota(jnp.int32, low.shape, 1)
    return jnp.where(place < threshold * 64, low, high)


def fill_left(left_ref, store, first_row, threshold, order):
    for row in range(store.shape[1]):
        pad = jnp.zeros((64, 512), store.dtype)
        blocks = [pad] + [store[h, row] for h in range(store.shape[0])] + [pad]
        dense = spread(blocks, 8 - first_row - row, WINDOWS * 8, threshold(first_row + row))
        for window in range(WINDOWS):
            at = pl.ds(pl.multiple_of(order(window) * 512, 512), 512)
            left_ref[row * 64:(row + 1) * 64, at] = dense[:, window * 512:(window + 1) * 512]


def collect(store, items, dest, valid):
    for number, item in enumerate(items):
        @pl.when(dest(number) >= 0)
        def _():
            store[dest(number)] = item[...]
    for place in range(store.shape[0]):
        @pl.when(valid(place) == 0)
        def _():
            store[place] = jnp.zeros(store.shape[1:], store.dtype)


def zero_invalid(store, valid):
    for place in range(store.shape[0]):
        @pl.when(valid(place) == 0)
        def _():
            store[place] = jnp.zeros(store.shape[1:], store.dtype)


def collected(items, store, sems, dest):
    copies = []
    for number, item in enumerate(items):
        place = dest(number)
        copy = pltpu.make_async_copy(item, store.at[jnp.maximum(place, 0)], sems.at[number])
        copies.append((place >= 0, copy))
    return copies


def start_all(copies):
    for needed, copy in copies:
        pl.when(needed)(copy.start)


def wait_all(copies):
    for needed, copy in copies:
        pl.when(needed)(copy.wait)


def windows(store, table_ref, count, threshold):
    row_count = store.shape[1]
    for window in range(count):
        for row in range(row_count):
            blocks = [store[window * PIECES + piece, row] for piece in range(PIECES)]
            at = window * 512 + row * 64
            table_ref[at:at + 64, :] = spread(blocks, 8 - row, 16, threshold(window * 8 + row))


def product(left_ref, table_ref, total_ref, before_ref=None):
    value = jnp.dot(left_ref[...], table_ref[...], preferred_element_type=jnp.float32)
    total_ref[...] = value if before_ref is None else before_ref[...] + value


def transfers(pairs, sems):
    copies = [pltpu.make_async_copy(source, target, sems.at[n]) for n, (source, target) in enumerate(pairs)]
    for copy in copies:
        copy.start()
    return copies


def own_kernel(meta_ref, dest_ref, *refs):
    items = refs[:4]
    left_near_out, left_far_out, table_out, total_out = refs[4:8]
    left_store, left, left_near, left_far, store, table, total, sems, out_sems = refs[8:]
    row_count = left_store.shape[1]
    copies = transfers([(items[n], left_store.at[dest_ref[4 + n]]) for n in range(4)], sems)
    zero_invalid(store, lambda p: dest_ref[8 + p])
    for copy in copies:
        copy.wait()
    for number in range(4):
        @pl.when(dest_ref[number] >= 0)
        def _():
            store[dest_ref[number]] = left_store[dest_ref[4 + number]]
    for row in range(row_count):
        pad = jnp.zeros((64, 512), left.dtype)
        blocks = [pad] + [left_store[h, row] for h in range(4)] + [pad]
        dense = spread(blocks, 8 - row, WINDOWS * 8, meta_ref[row])
        rows = slice(row * 64, (row + 1) * 64)
        left[rows, :] = dense[:, 1024:1536]
        left_far[rows, 512:1024] = dense[:, :512]
        left_far[rows, 1024:] = dense[:, 2048:]

        @pl.when(meta_ref[30] > 0)
        def _():
            left_near[rows, :] = dense[:, 1536:2048]
            left_far[rows, :512] = dense[:, 512:1024]

        @pl.when(meta_ref[30] < 0)
        def _():
            left_near[rows, :] = dense[:, 512:1024]
            left_far[rows, :512] = dense[:, 1536:2048]
    outs = transfers([(left_near, left_near_out), (left_far, left_far_out)], out_sems)
    windows(store, table, 1, lambda at: dest_ref[11 + at])
    outs += transfers([(table, table_out)], out_sems.at[pl.ds(2, 1)])
    product(left, table, total)
    outs += transfers([(total, total_out)], out_sems.at[pl.ds(3, 1)])
    for copy in outs:
        copy.wait()


def near_kernel(meta_ref, dest_ref, left_in, before_in, *refs):
    items = refs[:4]
    table_out, base_out, store, left, before, table, total, base, sems, in_sems, out_sems = refs[4:]
    copies = collected(items, store, sems, lambda n: dest_ref[n])
    start_all(copies)
    ins = transfers([(left_in, left), (before_in, before)], in_sems)
    zero_invalid(store, lambda p: dest_ref[4 + p])
    wait_all(copies)
    windows(store, table, 1, lambda at: dest_ref[7 + at])
    outs = transfers([(table, table_out)], out_sems)
    for copy in ins:
        copy.wait()
    product(left, table, total, before)
    for row in range(base.shape[0]):
        base[row] = kept(total[row * 64:(row + 1) * 64, :], row, meta_ref[8 + row], 512)
    outs += transfers([(base, base_out)], out_sems.at[pl.ds(1, 1)])
    for copy in outs:
        copy.wait()


def far_kernel(meta_ref, dest_ref, left_ref, base_ref, *refs):
    items = refs[:9]
    table_ref, square_ref, low_a, low_b, store, total_ref = refs[9:]
    row_count = items[0].shape[0]
    half = row_count // 2
    collect(store, items, lambda n: dest_ref[n], lambda p: dest_ref[9 + p])
    for window in range(3):
        for row in range(row_count):
            blocks = [store[window * PIECES + piece, row] for piece in range(PIECES)]
            at = window * 512 + row * 64
            table_ref[at:at + 64, :] = spread(blocks, 8 - row, 16, dest_ref[18 + window * 8 + row])

    product(left_ref, table_ref, total_ref)
    for row in range(row_count):
        picked = base_ref[row] + kept(total_ref[row * 64:(row + 1) * 64, :], row, meta_ref[8 + row], 512)
        square_ref[row] = picked
        low_ref = low_a if row < half else low_b
        low_ref[row % half] = picked.astype(low_ref.dtype)


def cube_kernel(part, meta_ref, own_ref, core_ref, x_ref, far_ref, table_own, table_near, table_b, square_ref, *refs):
    out_ref, store, left_ref, total_ref, result, sem = refs[part:]
    row_count = result.shape[0]
    first_row = part * row_count
    group = meta_ref[29]
    for bits, ref in enumerate((own_ref, core_ref, x_ref, far_ref)):
        store[group ^ bits] = ref[...]
    fill_left(left_ref, store, first_row, lambda row: meta_ref[16 + row], lambda window: meta_ref[24 + window])

    total_ref[...] = (
        jnp.dot(left_ref[:, :512], table_own[...], preferred_element_type=jnp.float32)
        + jnp.dot(left_ref[:, 512:1024], table_near[...], preferred_element_type=jnp.float32)
        + jnp.dot(left_ref[:, 1024:], table_b[...], preferred_element_type=jnp.float32)
    )
    for row in range(row_count):
        whole = first_row + row
        cube = kept(total_ref[row * 64:(row + 1) * 64, :], whole, meta_ref[8 + whole], 512)
        result[row] = (3.0 * square_ref[whole] - 2.0 * cube).astype(result.dtype)
    copy = pltpu.make_async_copy(result, out_ref.at[pl.ds(first_row, row_count)], sem)
    copy.start()
    copy.wait()


def missing_places(index, rows, total_rows, reach):
    places = (index - rows[:, None] + reach) % total_rows
    slots = jnp.arange(index.shape[1], dtype=jnp.int32)[None, :]
    return jnp.sum((places == slots).astype(jnp.int32), axis=1)


def per_device(dom_count, ka_count, x_blocks, col_index, prod_index):
    row_count, block, width = x_blocks.shape
    reach = 2 * row_count
    total_rows = row_count * dom_count
    dom = lax.axis_index("dom")
    group = lax.axis_index("ka")
    x_side, y_side = group // 2, dom % 2
    sign = 2 * x_side - 1
    same = x_side == y_side
    other = jnp.logical_not(same)
    near = 1 - 2 * y_side
    route = routes(dom_count, ka_count)
    steps = jnp.arange(row_count, dtype=jnp.int32)

    def missing(index, delta):
        there = (dom + delta) % dom_count * row_count + steps
        return missing_places(index, there, total_rows, reach)

    def along(value, source):
        return lax.ppermute(value, "dom", [(source(d) % dom_count, d) for d in range(dom_count)])

    from_near = along(col_index, lambda d: d ^ 1)
    from_far = along(col_index, lambda d: d + 1 if d % 2 else d - 1)
    from_before = along(col_index, lambda d: d - 2)
    from_after = along(col_index, lambda d: d + 2)
    own = x_blocks
    za = permuted(own, route["za"])
    zb = permuted(own, route["zb"])
    ox = permuted(own, route["x"])
    oy = permuted(own, route["y"])
    dd = permuted(own, route["dd"])
    own_core = permuted(own, route["core"])
    ox_core = permuted(ox, route["core"])
    oy_core = permuted(oy, route["core_oy"])
    from_near, dd = lax.optimization_barrier((from_near, dd))
    dd_core = permuted(dd, route["core_dd"])
    bx = permuted(za, route["x"])
    by_source = jnp.where(same, za, zb)
    z_source = jnp.where((group == 0) | (group == 3), za, zb)
    by = permuted(by_source, route["y"])
    z_core = permuted(z_source, route["core"])
    from_far, from_before, from_after, bx = lax.optimization_barrier((from_far, from_before, from_after, bx))
    bx_core = permuted(bx, route["core"])
    by_core = permuted(by, route["core_by"])

    place = {0: missing(col_index, 0), "near": missing(from_near, near), "far": missing(from_far, -near),
             -2: missing(from_before, -2), 2: missing(from_after, 2)}
    prod_place = missing(prod_index, 0)

    def dest_of(entries, window_of):
        out = []
        for delta, shard, valid in entries:
            piece = shard - group + delta + 1
            ok = valid & (piece >= 0) & (piece < PIECES)
            out.append(jnp.where(ok, window_of(delta) * PIECES + piece, -1))
        return out

    def valid_of(delta):
        shards = [group - delta - 1 + piece for piece in range(PIECES)]
        return [((shard >= 0) & (shard < ka_count)).astype(jnp.int32) for shard in shards]

    def threshold(delta, key):
        return place[key] - 8 * (group - delta) + steps

    def table_of(scalars, vectors):
        return jnp.concatenate([jnp.stack(scalars)] + vectors).astype(jnp.int32)

    order = [jnp.int32(3), 2 - (near == -1), jnp.int32(0), 2 - (near == 1), jnp.int32(4)]
    meta = jnp.concatenate(
        [place[0] + steps, prod_place - 8 * group, prod_place + steps, jnp.stack(order + [group, near])]
    ).astype(jnp.int32)

    yes = jnp.bool_(True)
    own_items = (own, own_core, ox, ox_core)
    own_table = table_of(
        dest_of([(0, group ^ bits, yes) for bits in range(4)], lambda delta: 0)
        + [group ^ bits for bits in range(4)] + valid_of(0),
        [threshold(0, 0)],
    )
    near_items = (oy, oy_core, dd, dd_core)
    near_table = table_of(
        dest_of(
            [(near, group, yes), (near, group ^ 1, yes), (near, group ^ 2, other), (near, group ^ 3, other)],
            lambda delta: 0,
        )
        + valid_of(near),
        [threshold(near, "near")],
    )
    far_items = (za, zb, z_core, bx, bx_core, by, by_core, dd, dd_core)
    far_dest = dest_of(
        [
            (-2 * sign, group, yes),
            (2 * sign, group, yes),
            (jnp.where((group == 0) | (group == 2), -2, 2), group ^ 1, yes),
            (2 * sign, group ^ 2, yes),
            (2 * sign, group ^ 3, yes),
            (-near, group, yes),
            (-near, group ^ 1, yes),
            (-near, group ^ 2, same),
            (-near, group ^ 3, same),
        ],
        lambda delta: jnp.where(delta == -2, 1, jnp.where(delta == 2, 2, 0)),
    )
    far_table = table_of(
        far_dest + valid_of(-near) + valid_of(-2) + valid_of(2),
        [threshold(-near, "far"), threshold(-2, -2), threshold(2, 2)],
    )

    smem = pl.BlockSpec(memory_space=pltpu.SMEM)
    vmem = pl.BlockSpec(memory_space=pltpu.VMEM)
    hbm = pl.BlockSpec(memory_space=pltpu.HBM)
    shards = (row_count, block, width)
    rows, depth, columns = row_count * block, WINDOWS * 8 * block, 16 * block
    shape = jax.ShapeDtypeStruct
    bf16, f32 = jnp.bfloat16, jnp.float32

    small = pltpu.CompilerParams(vmem_limit_bytes=28 << 20)

    def cost(k):
        return pl.CostEstimate(flops=2 * rows * k * columns * 2, bytes_accessed=12 << 20, transcendentals=0)

    def in_hbm(*values):
        return [pltpu.with_memory_space_constraint(value, pltpu.HBM) for value in values]

    dma = pltpu.SemaphoreType.DMA
    left_near, left_far, table_own, total = pl.pallas_call(
        own_kernel,
        out_shape=(
            pltpu.HBM((rows, 512), bf16),
            pltpu.HBM((rows, 1536), bf16),
            pltpu.HBM((512, columns), bf16),
            pltpu.HBM((rows, columns), f32),
        ),
        in_specs=[smem, smem] + [hbm] * 4,
        out_specs=(hbm,) * 4,
        scratch_shapes=[
            pltpu.VMEM((ka_count,) + shards, bf16),
            pltpu.VMEM((rows, 512), bf16),
            pltpu.VMEM((rows, 512), bf16),
            pltpu.VMEM((rows, 1536), bf16),
            pltpu.VMEM((PIECES,) + shards, bf16),
            pltpu.VMEM((512, columns), bf16),
            pltpu.VMEM((rows, columns), f32),
            dma((4,)),
            dma((4,)),
        ],
        compiler_params=small,
        cost_estimate=cost(512),
    )(meta, own_table, *in_hbm(*own_items))

    table_near, base = pl.pallas_call(
        near_kernel,
        out_shape=(pltpu.HBM((512, columns), bf16), pltpu.HBM(shards, f32)),
        in_specs=[smem, smem] + [hbm] * 6,
        out_specs=(hbm, hbm),
        scratch_shapes=[
            pltpu.VMEM((PIECES,) + shards, bf16),
            pltpu.VMEM((rows, 512), bf16),
            pltpu.VMEM((rows, columns), f32),
            pltpu.VMEM((512, columns), bf16),
            pltpu.VMEM((rows, columns), f32),
            pltpu.VMEM(shards, f32),
            dma((4,)),
            dma((2,)),
            dma((2,)),
        ],
        compiler_params=small,
        cost_estimate=cost(512),
    )(meta, near_table, *in_hbm(left_near, total, *near_items))

    half_rows = row_count // 2
    table_b, square, low_a, low_b = pl.pallas_call(
        far_kernel,
        out_shape=(
            shape((1536, columns), bf16),
            shape((row_count, block, width), f32),
            shape((half_rows, block, width), bf16),
            shape((half_rows, block, width), bf16),
        ),
        in_specs=[smem, smem] + [vmem] * 11,
        out_specs=(vmem, vmem, vmem, vmem),
        scratch_shapes=[
            pltpu.VMEM((3 * PIECES, row_count, block, width), bf16),
            pltpu.VMEM((rows, columns), f32),
        ],
        compiler_params=small,
        cost_estimate=cost(1536),
    )(meta, far_table, *[pltpu.with_memory_space_constraint(v, pltpu.HBM) for v in (left_far, base, za, zb)],
      *far_items[2:7], *[pltpu.with_memory_space_constraint(v, pltpu.HBM) for v in (dd, dd_core)])

    lows = (low_a, low_b)
    by_x = [permuted(low, route["x"]) for low in lows]
    by_partner = [permuted(low, route["core"]) for low in lows]
    by_both = [permuted(low, route["core"]) for low in by_x]
    out = ()
    for part in range(2):
        out = (pl.pallas_call(
            functools.partial(cube_kernel, part),
            out_shape=pltpu.HBM((row_count, block, width), bf16),
            in_specs=[smem] + [vmem] * 8 + [hbm] * part,
            out_specs=hbm,
            scratch_shapes=[
                pltpu.VMEM((ka_count, half_rows, block, width), bf16),
                pltpu.VMEM((rows // 2, depth), bf16),
                pltpu.VMEM((rows // 2, columns), f32),
                pltpu.VMEM((half_rows, block, width), bf16),
                pltpu.SemaphoreType.DMA,
            ],
            input_output_aliases={9: 0} if part else {},
            compiler_params=small,
            cost_estimate=cost(1280),
        )(meta, lows[part], by_partner[part], by_x[part], by_both[part],
          table_own, table_near, table_b, square, *out),)
    return out[0]


def solution(mesh):
    def body(*args):
        return per_device(mesh.shape["dom"], mesh.shape["ka"], *args)

    return jax.shard_map(
        body,
        mesh=mesh,
        in_specs=(P("dom", None, "ka"), P("dom", None), P("dom", None)),
        out_specs=P("dom", None, "ka"),
        check_vma=False,
    )
```

```python
import functools

import jax
import jax.numpy as jnp
from jax import lax
from jax.experimental import pallas as pl
from jax.experimental.pallas import tpu as pltpu
from jax.sharding import PartitionSpec as P


WINDOWS = 5
PIECES = 3


def permuted(value, pairs):
    return lax.ppermute(value, ("dom", "ka"), pairs)


def routes(dom_count, ka_count):
    def pairs(target):
        out = []
        for dom in range(dom_count):
            for group in range(ka_count):
                to = target(dom, group, group // 2, dom % 2)
                if to is not None:
                    out.append((dom * ka_count + group, (to[0] % dom_count) * ka_count + to[1]))
        return out

    def core(takers):
        return pairs(lambda d, g, x, y: (d, g ^ 1) if (g ^ 1) in takers(x, y) else None)

    return {
        "za": pairs(lambda d, g, x, y: (d + 2 if x else d - 2, g)),
        "zb": pairs(lambda d, g, x, y: (d - 2 if x else d + 2, g) if x != y or g in (1, 2) else None),
        "x": pairs(lambda d, g, x, y: (d, g ^ 2)),
        "y": pairs(lambda d, g, x, y: (d ^ 1, g)),
        "dd": pairs(lambda d, g, x, y: (d + 1 if x else d - 1, g ^ 2)),
        "core": core(lambda x, y: (0, 1, 2, 3)),
        "core_dd": core(lambda x, y: (1, 2)),
        "core_oy": core(lambda x, y: ((1, 0), (3, 2))[x][y:y + 1]),
        "core_by": core(lambda x, y: ((0, 1), (2, 3))[x][y:y + 1]),
    }


def spread(pieces, shift, width, threshold):
    wide = jnp.concatenate(pieces, axis=1)
    low = wide[:, shift * 64:(shift + width) * 64]
    high = wide[:, (shift - 1) * 64:(shift - 1 + width) * 64]
    place = lax.broadcasted_iota(jnp.int32, low.shape, 1)
    zero = jnp.zeros_like(low)
    return jnp.where(place < threshold * 64, low, jnp.where(place >= threshold * 64 + 64, high, zero))


def kept(total, row, threshold, width):
    low = total[:, row * 64:row * 64 + width]
    high = total[:, (row + 1) * 64:(row + 1) * 64 + width]
    place = lax.broadcasted_iota(jnp.int32, low.shape, 1)
    return jnp.where(place < threshold * 64, low, high)


def fill_left(left_ref, store, first_row, threshold, order):
    for row in range(store.shape[1]):
        pad = jnp.zeros((64, 512), store.dtype)
        blocks = [pad] + [store[h, row] for h in range(store.shape[0])] + [pad]
        dense = spread(blocks, 8 - first_row - row, WINDOWS * 8, threshold(first_row + row))
        for window in range(WINDOWS):
            at = pl.ds(pl.multiple_of(order(window) * 512, 512), 512)
            left_ref[row * 64:(row + 1) * 64, at] = dense[:, window * 512:(window + 1) * 512]


def collect(store, items, firsts, dest, valid):
    for number, item in enumerate(items):
        @pl.when(dest(number) >= 0)
        def _():
            store[dest(number), firsts[number]:firsts[number] + item.shape[0]] = item[...]
    for place in range(store.shape[0]):
        @pl.when(valid(place) == 0)
        def _():
            store[place] = jnp.zeros(store.shape[1:], store.dtype)


def zero_invalid(store, valid):
    for place in range(store.shape[0]):
        @pl.when(valid(place) == 0)
        def _():
            store[place] = jnp.zeros(store.shape[1:], store.dtype)


def collected(items, store, sems, dest):
    copies = []
    for number, item in enumerate(items):
        place = dest(number)
        copy = pltpu.make_async_copy(item, store.at[jnp.maximum(place, 0)], sems.at[number])
        copies.append((place >= 0, copy))
    return copies


def start_all(copies):
    for needed, copy in copies:
        pl.when(needed)(copy.start)


def wait_all(copies):
    for needed, copy in copies:
        pl.when(needed)(copy.wait)


def windows(store, table_ref, count, threshold):
    row_count = store.shape[1]
    for window in range(count):
        for row in range(row_count):
            blocks = [store[window * PIECES + piece, row] for piece in range(PIECES)]
            at = window * 512 + row * 64
            table_ref[at:at + 64, :] = spread(blocks, 8 - row, 16, threshold(window * 8 + row))


def product(left_ref, table_ref, total_ref, before_ref=None):
    value = jnp.dot(left_ref[...], table_ref[...], preferred_element_type=jnp.float32)
    total_ref[...] = value if before_ref is None else before_ref[...] + value


def transfers(pairs, sems):
    copies = [pltpu.make_async_copy(source, target, sems.at[n]) for n, (source, target) in enumerate(pairs)]
    for copy in copies:
        copy.start()
    return copies


def own_kernel(meta_ref, dest_ref, *refs):
    items = refs[:4]
    left_near_out, left_far_0, left_far_1, table_out, total_out = refs[4:9]
    left_store, left, left_near, left_far, store, table, total, sems, out_sems = refs[9:]
    row_count = left_store.shape[1]
    half = left_far.shape[0] // 2
    copies = transfers([(items[n], left_store.at[dest_ref[4 + n]]) for n in range(4)], sems)
    zero_invalid(store, lambda p: dest_ref[8 + p])
    for copy in copies:
        copy.wait()
    for number in range(4):
        @pl.when(dest_ref[number] >= 0)
        def _():
            store[dest_ref[number]] = left_store[dest_ref[4 + number]]
    for row in range(row_count):
        pad = jnp.zeros((64, 512), left.dtype)
        blocks = [pad] + [left_store[h, row] for h in range(4)] + [pad]
        dense = spread(blocks, 8 - row, WINDOWS * 8, meta_ref[row])
        rows = slice(row * 64, (row + 1) * 64)
        left[rows, :] = dense[:, 1024:1536]
        left_far[rows, 512:1024] = dense[:, :512]
        left_far[rows, 1024:] = dense[:, 2048:]

        @pl.when(meta_ref[30] > 0)
        def _():
            left_near[rows, :] = dense[:, 1536:2048]
            left_far[rows, :512] = dense[:, 512:1024]

        @pl.when(meta_ref[30] < 0)
        def _():
            left_near[rows, :] = dense[:, 512:1024]
            left_far[rows, :512] = dense[:, 1536:2048]
    outs = transfers([(left_near, left_near_out), (left_far.at[pl.ds(0, half)], left_far_0),
                      (left_far.at[pl.ds(half, half)], left_far_1)], out_sems)
    windows(store, table, 1, lambda at: dest_ref[11 + at])
    outs += transfers([(table, table_out)], out_sems.at[pl.ds(3, 1)])
    product(left, table, total)
    outs += transfers([(total, total_out)], out_sems.at[pl.ds(4, 1)])
    for copy in outs:
        copy.wait()


def near_kernel(meta_ref, dest_ref, left_in, before_in, *refs):
    items = refs[:4]
    table_out, base_0, base_1, store, left, before, table, total, base, sems, in_sems, out_sems = refs[4:]
    half = base.shape[0] // 2
    copies = collected(items, store, sems, lambda n: dest_ref[n])
    start_all(copies)
    ins = transfers([(left_in, left), (before_in, before)], in_sems)
    zero_invalid(store, lambda p: dest_ref[4 + p])
    wait_all(copies)
    windows(store, table, 1, lambda at: dest_ref[7 + at])
    outs = transfers([(table, table_out)], out_sems)
    for copy in ins:
        copy.wait()
    product(left, table, total, before)
    for row in range(base.shape[0]):
        base[row] = kept(total[row * 64:(row + 1) * 64, :], row, meta_ref[8 + row], 512)
    outs += transfers([(base.at[pl.ds(0, half)], base_0), (base.at[pl.ds(half, half)], base_1)], out_sems.at[pl.ds(1, 2)])
    for copy in outs:
        copy.wait()


def far_kernel(meta_ref, dest_ref, left_ref, base_ref, *refs):
    items = refs[:11]
    table_ref, square_ref, low_ref, store, total_ref = refs[11:]
    row_count = items[0].shape[0]
    half = row_count // 2
    firsts = (0,) * 7 + (half,) * 2 + (0,) * 2
    collect(store, items, firsts, lambda n: dest_ref[n], lambda p: dest_ref[11 + p])
    for window in range(3):
        for row in range(row_count):
            blocks = [store[window * PIECES + piece, row] for piece in range(PIECES)]
            at = window * 512 + row * 64
            table_ref[at:at + 64, :] = spread(blocks, 8 - row, 16, dest_ref[20 + window * 8 + row])

    squares(meta_ref, 0, left_ref, base_ref, table_ref, square_ref, low_ref, total_ref)


def squares(meta_ref, part, left_ref, base_ref, table_ref, square_ref, low_ref, total_ref):
    product(left_ref, table_ref, total_ref)
    for row in range(square_ref.shape[0]):
        whole = part * square_ref.shape[0] + row
        picked = base_ref[row] + kept(total_ref[row * 64:(row + 1) * 64, :], whole, meta_ref[8 + whole], 512)
        square_ref[row] = picked
        low_ref[row] = picked.astype(low_ref.dtype)


def second_kernel(meta_ref, left_ref, base_ref, table_ref, square_ref, low_ref, total_ref):
    squares(meta_ref, 1, left_ref, base_ref, table_ref, square_ref, low_ref, total_ref)


def cube_kernel(part, meta_ref, own_ref, core_ref, x_ref, far_ref, table_own, table_near, table_b, square_ref, *refs):
    out_ref, store, left_ref, total_ref, result, sem = refs[part:]
    row_count = result.shape[0]
    first_row = part * row_count
    group = meta_ref[29]
    for bits, ref in enumerate((own_ref, core_ref, x_ref, far_ref)):
        store[group ^ bits] = ref[...]
    fill_left(left_ref, store, first_row, lambda row: meta_ref[16 + row], lambda window: meta_ref[24 + window])

    total_ref[...] = (
        jnp.dot(left_ref[:, :512], table_own[...], preferred_element_type=jnp.float32)
        + jnp.dot(left_ref[:, 512:1024], table_near[...], preferred_element_type=jnp.float32)
        + jnp.dot(left_ref[:, 1024:], table_b[...], preferred_element_type=jnp.float32)
    )
    for row in range(row_count):
        whole = first_row + row
        cube = kept(total_ref[row * 64:(row + 1) * 64, :], whole, meta_ref[8 + whole], 512)
        result[row] = (3.0 * square_ref[row] - 2.0 * cube).astype(result.dtype)
    copy = pltpu.make_async_copy(result, out_ref.at[pl.ds(first_row, row_count)], sem)
    copy.start()
    copy.wait()


def missing_places(index, rows, total_rows, reach):
    places = (index - rows[:, None] + reach) % total_rows
    slots = jnp.arange(index.shape[1], dtype=jnp.int32)[None, :]
    return jnp.sum((places == slots).astype(jnp.int32), axis=1)


def per_device(dom_count, ka_count, x_blocks, col_index, prod_index):
    row_count, block, width = x_blocks.shape
    reach = 2 * row_count
    total_rows = row_count * dom_count
    dom = lax.axis_index("dom")
    group = lax.axis_index("ka")
    x_side, y_side = group // 2, dom % 2
    sign = 2 * x_side - 1
    same = x_side == y_side
    other = jnp.logical_not(same)
    near = 1 - 2 * y_side
    route = routes(dom_count, ka_count)
    steps = jnp.arange(row_count, dtype=jnp.int32)

    def missing(index, delta):
        there = (dom + delta) % dom_count * row_count + steps
        return missing_places(index, there, total_rows, reach)

    def along(value, source):
        return lax.ppermute(value, "dom", [(source(d) % dom_count, d) for d in range(dom_count)])

    from_near = along(col_index, lambda d: d ^ 1)
    from_far = along(col_index, lambda d: d + 1 if d % 2 else d - 1)
    from_before = along(col_index, lambda d: d - 2)
    from_after = along(col_index, lambda d: d + 2)
    own = x_blocks
    za = permuted(own, route["za"])
    zb = permuted(own, route["zb"])
    ox = permuted(own, route["x"])
    oy = permuted(own, route["y"])
    dd = permuted(own, route["dd"])
    own_core = permuted(own, route["core"])
    ox_core = permuted(ox, route["core"])
    oy_core = permuted(oy, route["core_oy"])
    from_near, dd = lax.optimization_barrier((from_near, dd))
    dd_core = permuted(dd, route["core_dd"])
    bx = permuted(za, route["x"])
    half_rows = row_count // 2
    by_source = [jnp.where(same, za[first:first + half_rows], zb[first:first + half_rows]) for first in (0, half_rows)]
    z_source = jnp.where((group == 0) | (group == 3), za, zb)
    by_0 = permuted(by_source[0], route["y"])
    by_1 = permuted(by_source[1], route["y"])
    z_core = permuted(z_source, route["core"])
    from_far, from_before, from_after, bx = lax.optimization_barrier((from_far, from_before, from_after, bx))
    bx_core = permuted(bx, route["core"])
    by_0_core = permuted(by_0, route["core_by"])
    by_1_core = permuted(by_1, route["core_by"])

    place = {0: missing(col_index, 0), "near": missing(from_near, near), "far": missing(from_far, -near),
             -2: missing(from_before, -2), 2: missing(from_after, 2)}
    prod_place = missing(prod_index, 0)

    def dest_of(entries, window_of):
        out = []
        for delta, shard, valid in entries:
            piece = shard - group + delta + 1
            ok = valid & (piece >= 0) & (piece < PIECES)
            out.append(jnp.where(ok, window_of(delta) * PIECES + piece, -1))
        return out

    def valid_of(delta):
        shards = [group - delta - 1 + piece for piece in range(PIECES)]
        return [((shard >= 0) & (shard < ka_count)).astype(jnp.int32) for shard in shards]

    def threshold(delta, key):
        return place[key] - 8 * (group - delta) + steps

    def table_of(scalars, vectors):
        return jnp.concatenate([jnp.stack(scalars)] + vectors).astype(jnp.int32)

    order = [jnp.int32(3), 2 - (near == -1), jnp.int32(0), 2 - (near == 1), jnp.int32(4)]
    meta = jnp.concatenate(
        [place[0] + steps, prod_place - 8 * group, prod_place + steps, jnp.stack(order + [group, near])]
    ).astype(jnp.int32)

    yes = jnp.bool_(True)
    own_items = (own, own_core, ox, ox_core)
    own_table = table_of(
        dest_of([(0, group ^ bits, yes) for bits in range(4)], lambda delta: 0)
        + [group ^ bits for bits in range(4)] + valid_of(0),
        [threshold(0, 0)],
    )
    near_items = (oy, oy_core, dd, dd_core)
    near_table = table_of(
        dest_of(
            [(near, group, yes), (near, group ^ 1, yes), (near, group ^ 2, other), (near, group ^ 3, other)],
            lambda delta: 0,
        )
        + valid_of(near),
        [threshold(near, "near")],
    )
    far_items = (za, zb, z_core, bx, bx_core, by_0, by_0_core, by_1, by_1_core, dd, dd_core)
    far_dest = dest_of(
        [
            (-2 * sign, group, yes),
            (2 * sign, group, yes),
            (jnp.where((group == 0) | (group == 2), -2, 2), group ^ 1, yes),
            (2 * sign, group ^ 2, yes),
            (2 * sign, group ^ 3, yes),
            (-near, group, yes),
            (-near, group ^ 1, yes),
            (-near, group, yes),
            (-near, group ^ 1, yes),
            (-near, group ^ 2, same),
            (-near, group ^ 3, same),
        ],
        lambda delta: jnp.where(delta == -2, 1, jnp.where(delta == 2, 2, 0)),
    )
    far_table = table_of(
        far_dest + valid_of(-near) + valid_of(-2) + valid_of(2),
        [threshold(-near, "far"), threshold(-2, -2), threshold(2, 2)],
    )

    smem = pl.BlockSpec(memory_space=pltpu.SMEM)
    vmem = pl.BlockSpec(memory_space=pltpu.VMEM)
    hbm = pl.BlockSpec(memory_space=pltpu.HBM)
    shards = (row_count, block, width)
    rows, depth, columns = row_count * block, WINDOWS * 8 * block, 16 * block
    shape = jax.ShapeDtypeStruct
    bf16, f32 = jnp.bfloat16, jnp.float32

    small = pltpu.CompilerParams(vmem_limit_bytes=28 << 20)

    def cost(k):
        return pl.CostEstimate(flops=2 * rows * k * columns * 2, bytes_accessed=12 << 20, transcendentals=0)

    def in_hbm(*values):
        return [pltpu.with_memory_space_constraint(value, pltpu.HBM) for value in values]

    dma = pltpu.SemaphoreType.DMA
    left_near, left_far_0, left_far_1, table_own, total = pl.pallas_call(
        own_kernel,
        out_shape=(
            pltpu.HBM((rows, 512), bf16),
            pltpu.HBM((rows // 2, 1536), bf16),
            pltpu.HBM((rows // 2, 1536), bf16),
            pltpu.HBM((512, columns), bf16),
            pltpu.HBM((rows, columns), f32),
        ),
        in_specs=[smem, smem] + [hbm] * 4,
        out_specs=(hbm,) * 5,
        scratch_shapes=[
            pltpu.VMEM((ka_count,) + shards, bf16),
            pltpu.VMEM((rows, 512), bf16),
            pltpu.VMEM((rows, 512), bf16),
            pltpu.VMEM((rows, 1536), bf16),
            pltpu.VMEM((PIECES,) + shards, bf16),
            pltpu.VMEM((512, columns), bf16),
            pltpu.VMEM((rows, columns), f32),
            dma((4,)),
            dma((5,)),
        ],
        compiler_params=small,
        cost_estimate=cost(512),
    )(meta, own_table, *in_hbm(*own_items))

    table_near, base_0, base_1 = pl.pallas_call(
        near_kernel,
        out_shape=(
            pltpu.HBM((512, columns), bf16),
            pltpu.HBM((row_count // 2, block, width), f32),
            pltpu.HBM((row_count // 2, block, width), f32),
        ),
        in_specs=[smem, smem] + [hbm] * 6,
        out_specs=(hbm, hbm, hbm),
        scratch_shapes=[
            pltpu.VMEM((PIECES,) + shards, bf16),
            pltpu.VMEM((rows, 512), bf16),
            pltpu.VMEM((rows, columns), f32),
            pltpu.VMEM((512, columns), bf16),
            pltpu.VMEM((rows, columns), f32),
            pltpu.VMEM(shards, f32),
            dma((4,)),
            dma((2,)),
            dma((3,)),
        ],
        compiler_params=small,
        cost_estimate=cost(512),
    )(meta, near_table, *in_hbm(left_near, total, *near_items))

    half_rows = row_count // 2
    half_shape = (half_rows, block, width)
    table_b, square_0, low_0 = pl.pallas_call(
        far_kernel,
        out_shape=(shape((1536, columns), bf16), shape(half_shape, f32), shape(half_shape, bf16)),
        in_specs=[smem, smem] + [vmem] * 13,
        out_specs=(vmem, vmem, vmem),
        scratch_shapes=[pltpu.VMEM((3 * PIECES, row_count, block, width), bf16), pltpu.VMEM((rows // 2, columns), f32)],
        compiler_params=small,
        cost_estimate=cost(1536),
    )(meta, far_table, *in_hbm(left_far_0, base_0, za, zb), *far_items[2:9], *in_hbm(dd, dd_core))
    square_1, low_1 = pl.pallas_call(
        second_kernel,
        out_shape=(shape(half_shape, f32), shape(half_shape, bf16)),
        in_specs=[smem] + [vmem] * 3,
        out_specs=(vmem, vmem),
        scratch_shapes=[pltpu.VMEM((rows // 2, columns), f32)],
        compiler_params=small,
        cost_estimate=cost(768),
    )(meta, *in_hbm(left_far_1, base_1), table_b)

    lows, square = (low_0, low_1), (square_0, square_1)
    by_x = [permuted(low, route["x"]) for low in lows]
    by_partner = [permuted(low, route["core"]) for low in lows]
    by_both = [permuted(low, route["core"]) for low in by_x]
    out = ()
    for part in range(2):
        out = (pl.pallas_call(
            functools.partial(cube_kernel, part),
            out_shape=pltpu.HBM((row_count, block, width), bf16),
            in_specs=[smem] + [vmem] * 8 + [hbm] * part,
            out_specs=hbm,
            scratch_shapes=[
                pltpu.VMEM((ka_count, half_rows, block, width), bf16),
                pltpu.VMEM((rows // 2, depth), bf16),
                pltpu.VMEM((rows // 2, columns), f32),
                pltpu.VMEM((half_rows, block, width), bf16),
                pltpu.SemaphoreType.DMA,
            ],
            input_output_aliases={9: 0} if part else {},
            compiler_params=small,
            cost_estimate=cost(1280),
        )(meta, lows[part], by_partner[part], by_x[part], by_both[part],
          table_own, table_near, table_b, square[part], *out),)
    return out[0]


def solution(mesh):
    def body(*args):
        return per_device(mesh.shape["dom"], mesh.shape["ka"], *args)

    return jax.shard_map(
        body,
        mesh=mesh,
        in_specs=(P("dom", None, "ka"), P("dom", None), P("dom", None)),
        out_specs=P("dom", None, "ka"),
        check_vma=False,
    )
```

```python
import functools

import jax
import jax.numpy as jnp
from jax import lax
from jax.experimental import pallas as pl
from jax.experimental.pallas import tpu as pltpu
from jax.sharding import PartitionSpec as P


WINDOWS = 5
PIECES = 3


def permuted(value, pairs):
    return lax.ppermute(value, ("dom", "ka"), pairs)


def routes(dom_count, ka_count):
    def pairs(target):
        out = []
        for dom in range(dom_count):
            for group in range(ka_count):
                to = target(dom, group, group // 2, dom % 2)
                if to is not None:
                    out.append((dom * ka_count + group, (to[0] % dom_count) * ka_count + to[1]))
        return out

    def core(takers):
        return pairs(lambda d, g, x, y: (d, g ^ 1) if (g ^ 1) in takers(x, y) else None)

    return {
        "za": pairs(lambda d, g, x, y: (d + 2 if x else d - 2, g)),
        "zb": pairs(lambda d, g, x, y: (d - 2 if x else d + 2, g) if x != y or g in (1, 2) else None),
        "x": pairs(lambda d, g, x, y: (d, g ^ 2)),
        "y": pairs(lambda d, g, x, y: (d ^ 1, g)),
        "dd": pairs(lambda d, g, x, y: (d + 1 if x else d - 1, g ^ 2)),
        "core": core(lambda x, y: (0, 1, 2, 3)),
        "core_dd": core(lambda x, y: (1, 2)),
        "core_oy": core(lambda x, y: ((1, 0), (3, 2))[x][y:y + 1]),
        "core_by": core(lambda x, y: ((0, 1), (2, 3))[x][y:y + 1]),
    }


def spread(pieces, shift, width, threshold):
    wide = jnp.concatenate(pieces, axis=1)
    low = wide[:, shift * 64:(shift + width) * 64]
    high = wide[:, (shift - 1) * 64:(shift - 1 + width) * 64]
    place = lax.broadcasted_iota(jnp.int32, low.shape, 1)
    zero = jnp.zeros_like(low)
    return jnp.where(place < threshold * 64, low, jnp.where(place >= threshold * 64 + 64, high, zero))


def kept(total, row, threshold, width):
    low = total[:, row * 64:row * 64 + width]
    high = total[:, (row + 1) * 64:(row + 1) * 64 + width]
    place = lax.broadcasted_iota(jnp.int32, low.shape, 1)
    return jnp.where(place < threshold * 64, low, high)


def fill_left(left_ref, store, first_row, threshold, order):
    for row in range(store.shape[1]):
        pad = jnp.zeros((64, 512), store.dtype)
        blocks = [pad] + [store[h, row] for h in range(store.shape[0])] + [pad]
        dense = spread(blocks, 8 - first_row - row, WINDOWS * 8, threshold(first_row + row))
        for window in range(WINDOWS):
            at = pl.ds(pl.multiple_of(order(window) * 512, 512), 512)
            left_ref[row * 64:(row + 1) * 64, at] = dense[:, window * 512:(window + 1) * 512]


def collect(store, items, firsts, dest, valid):
    for number, item in enumerate(items):
        @pl.when(dest(number) >= 0)
        def _():
            store[dest(number), firsts[number]:firsts[number] + item.shape[0]] = item[...]
    for place in range(store.shape[0]):
        @pl.when(valid(place) == 0)
        def _():
            store[place] = jnp.zeros(store.shape[1:], store.dtype)


def zero_invalid(store, valid):
    for place in range(store.shape[0]):
        @pl.when(valid(place) == 0)
        def _():
            store[place] = jnp.zeros(store.shape[1:], store.dtype)


def collected(items, store, sems, dest):
    copies = []
    for number, item in enumerate(items):
        place = dest(number)
        copy = pltpu.make_async_copy(item, store.at[jnp.maximum(place, 0)], sems.at[number])
        copies.append((place >= 0, copy))
    return copies


def start_all(copies):
    for needed, copy in copies:
        pl.when(needed)(copy.start)


def wait_all(copies):
    for needed, copy in copies:
        pl.when(needed)(copy.wait)


def windows(store, table_ref, count, threshold):
    row_count = store.shape[1]
    for window in range(count):
        for row in range(row_count):
            blocks = [store[window * PIECES + piece, row] for piece in range(PIECES)]
            at = window * 512 + row * 64
            table_ref[at:at + 64, :] = spread(blocks, 8 - row, 16, threshold(window * 8 + row))


def product(left_ref, table_ref, total_ref, before_ref=None):
    value = jnp.dot(left_ref[...], table_ref[...], preferred_element_type=jnp.float32)
    total_ref[...] = value if before_ref is None else before_ref[...] + value


def transfers(pairs, sems):
    copies = [pltpu.make_async_copy(source, target, sems.at[n]) for n, (source, target) in enumerate(pairs)]
    for copy in copies:
        copy.start()
    return copies


def own_kernel(meta_ref, dest_ref, *refs):
    items = refs[:4]
    left_near_out, left_far_0, left_far_1, table_out, total_out = refs[4:9]
    left_store, left, left_near, left_far, store, table, total, sems, out_sems = refs[9:]
    row_count = left_store.shape[1]
    half = left_far.shape[0] // 2
    copies = transfers([(items[n], left_store.at[dest_ref[4 + n]]) for n in range(4)], sems)
    zero_invalid(store, lambda p: dest_ref[8 + p])
    for copy in copies:
        copy.wait()
    for number in range(4):
        @pl.when(dest_ref[number] >= 0)
        def _():
            store[dest_ref[number]] = left_store[dest_ref[4 + number]]
    for row in range(row_count):
        pad = jnp.zeros((64, 512), left.dtype)
        blocks = [pad] + [left_store[h, row] for h in range(4)] + [pad]
        dense = spread(blocks, 8 - row, WINDOWS * 8, meta_ref[row])
        rows = slice(row * 64, (row + 1) * 64)
        left[rows, :] = dense[:, 1024:1536]
        left_far[rows, 512:1024] = dense[:, :512]
        left_far[rows, 1024:] = dense[:, 2048:]

        @pl.when(meta_ref[30] > 0)
        def _():
            left_near[rows, :] = dense[:, 1536:2048]
            left_far[rows, :512] = dense[:, 512:1024]

        @pl.when(meta_ref[30] < 0)
        def _():
            left_near[rows, :] = dense[:, 512:1024]
            left_far[rows, :512] = dense[:, 1536:2048]
    outs = transfers([(left_near, left_near_out), (left_far.at[pl.ds(0, half)], left_far_0),
                      (left_far.at[pl.ds(half, half)], left_far_1)], out_sems)
    windows(store, table, 1, lambda at: dest_ref[11 + at])
    outs += transfers([(table, table_out)], out_sems.at[pl.ds(3, 1)])
    product(left, table, total)
    outs += transfers([(total, total_out)], out_sems.at[pl.ds(4, 1)])
    for copy in outs:
        copy.wait()


def near_kernel(meta_ref, dest_ref, left_in, before_in, *refs):
    items = refs[:4]
    table_out, base_0, base_1, store, left, before, table, total, base, sems, in_sems, out_sems = refs[4:]
    half = base.shape[0] // 2
    copies = collected(items, store, sems, lambda n: dest_ref[n])
    start_all(copies)
    ins = transfers([(left_in, left), (before_in, before)], in_sems)
    zero_invalid(store, lambda p: dest_ref[4 + p])
    wait_all(copies)
    windows(store, table, 1, lambda at: dest_ref[7 + at])
    outs = transfers([(table, table_out)], out_sems)
    for copy in ins:
        copy.wait()
    product(left, table, total, before)
    for row in range(base.shape[0]):
        base[row] = kept(total[row * 64:(row + 1) * 64, :], row, meta_ref[8 + row], 512)
    outs += transfers([(base.at[pl.ds(0, half)], base_0), (base.at[pl.ds(half, half)], base_1)], out_sems.at[pl.ds(1, 2)])
    for copy in outs:
        copy.wait()


def far_kernel(meta_ref, dest_ref, left_ref, base_ref, *refs):
    items = refs[:11]
    table_ref, square_ref, low_ref, store, total_ref, sems = refs[11:]
    row_count = items[0].shape[0]
    half = row_count // 2
    early = (0, 1, 9, 10)
    copies = collected([items[n] for n in early], store, sems, lambda n: dest_ref[early[n]])
    start_all(copies)
    firsts = (0,) * 5 + (half,) * 2
    collect(store, items[2:9], firsts, lambda n: dest_ref[2 + n], lambda p: dest_ref[11 + p])
    wait_all(copies)
    for window in range(3):
        for row in range(row_count):
            blocks = [store[window * PIECES + piece, row] for piece in range(PIECES)]
            at = window * 512 + row * 64
            table_ref[at:at + 64, :] = spread(blocks, 8 - row, 16, dest_ref[20 + window * 8 + row])

    squares(meta_ref, 0, left_ref, base_ref, table_ref, square_ref, low_ref, total_ref)


def squares(meta_ref, part, left_ref, base_ref, table_ref, square_ref, low_ref, total_ref):
    product(left_ref, table_ref, total_ref)
    for row in range(square_ref.shape[0]):
        whole = part * square_ref.shape[0] + row
        picked = base_ref[row] + kept(total_ref[row * 64:(row + 1) * 64, :], whole, meta_ref[8 + whole], 512)
        square_ref[row] = picked
        low_ref[row] = picked.astype(low_ref.dtype)


def second_kernel(meta_ref, left_ref, base_ref, table_ref, square_ref, low_ref, total_ref):
    squares(meta_ref, 1, left_ref, base_ref, table_ref, square_ref, low_ref, total_ref)


def cube_kernel(part, meta_ref, own_ref, core_ref, x_ref, far_ref, table_own, table_near, table_b, square_ref, *refs):
    out_ref, store, left_ref, total_ref, result, sem = refs[part:]
    row_count = result.shape[0]
    first_row = part * row_count
    group = meta_ref[29]
    for bits, ref in enumerate((own_ref, core_ref, x_ref, far_ref)):
        store[group ^ bits] = ref[...]
    fill_left(left_ref, store, first_row, lambda row: meta_ref[16 + row], lambda window: meta_ref[24 + window])

    total_ref[...] = (
        jnp.dot(left_ref[:, :512], table_own[...], preferred_element_type=jnp.float32)
        + jnp.dot(left_ref[:, 512:1024], table_near[...], preferred_element_type=jnp.float32)
        + jnp.dot(left_ref[:, 1024:], table_b[...], preferred_element_type=jnp.float32)
    )
    for row in range(row_count):
        whole = first_row + row
        cube = kept(total_ref[row * 64:(row + 1) * 64, :], whole, meta_ref[8 + whole], 512)
        result[row] = (3.0 * square_ref[row] - 2.0 * cube).astype(result.dtype)
    copy = pltpu.make_async_copy(result, out_ref.at[pl.ds(first_row, row_count)], sem)
    copy.start()
    copy.wait()


def missing_places(index, rows, total_rows, reach):
    places = (index - rows[:, None] + reach) % total_rows
    slots = jnp.arange(index.shape[1], dtype=jnp.int32)[None, :]
    return jnp.sum((places == slots).astype(jnp.int32), axis=1)


def per_device(dom_count, ka_count, x_blocks, col_index, prod_index):
    row_count, block, width = x_blocks.shape
    reach = 2 * row_count
    total_rows = row_count * dom_count
    dom = lax.axis_index("dom")
    group = lax.axis_index("ka")
    x_side, y_side = group // 2, dom % 2
    sign = 2 * x_side - 1
    same = x_side == y_side
    other = jnp.logical_not(same)
    near = 1 - 2 * y_side
    route = routes(dom_count, ka_count)
    steps = jnp.arange(row_count, dtype=jnp.int32)

    def missing(index, delta):
        there = (dom + delta) % dom_count * row_count + steps
        return missing_places(index, there, total_rows, reach)

    def along(value, source):
        return lax.ppermute(value, "dom", [(source(d) % dom_count, d) for d in range(dom_count)])

    from_near = along(col_index, lambda d: d ^ 1)
    from_far = along(col_index, lambda d: d + 1 if d % 2 else d - 1)
    from_before = along(col_index, lambda d: d - 2)
    from_after = along(col_index, lambda d: d + 2)
    own = x_blocks
    za = permuted(own, route["za"])
    zb = permuted(own, route["zb"])
    ox = permuted(own, route["x"])
    oy = permuted(own, route["y"])
    dd = permuted(own, route["dd"])
    own_core = permuted(own, route["core"])
    ox_core = permuted(ox, route["core"])
    oy_core = permuted(oy, route["core_oy"])
    from_near, dd = lax.optimization_barrier((from_near, dd))
    dd_core = permuted(dd, route["core_dd"])
    bx = permuted(za, route["x"])
    half_rows = row_count // 2
    by_source = [jnp.where(same, za[first:first + half_rows], zb[first:first + half_rows]) for first in (0, half_rows)]
    z_source = jnp.where((group == 0) | (group == 3), za, zb)
    by_0 = permuted(by_source[0], route["y"])
    by_1 = permuted(by_source[1], route["y"])
    z_core = permuted(z_source, route["core"])
    from_far, from_before, from_after, bx = lax.optimization_barrier((from_far, from_before, from_after, bx))
    bx_core = permuted(bx, route["core"])
    by_0_core = permuted(by_0, route["core_by"])
    by_1_core = permuted(by_1, route["core_by"])

    place = {0: missing(col_index, 0), "near": missing(from_near, near), "far": missing(from_far, -near),
             -2: missing(from_before, -2), 2: missing(from_after, 2)}
    prod_place = missing(prod_index, 0)

    def dest_of(entries, window_of):
        out = []
        for delta, shard, valid in entries:
            piece = shard - group + delta + 1
            ok = valid & (piece >= 0) & (piece < PIECES)
            out.append(jnp.where(ok, window_of(delta) * PIECES + piece, -1))
        return out

    def valid_of(delta):
        shards = [group - delta - 1 + piece for piece in range(PIECES)]
        return [((shard >= 0) & (shard < ka_count)).astype(jnp.int32) for shard in shards]

    def threshold(delta, key):
        return place[key] - 8 * (group - delta) + steps

    def table_of(scalars, vectors):
        return jnp.concatenate([jnp.stack(scalars)] + vectors).astype(jnp.int32)

    order = [jnp.int32(3), 2 - (near == -1), jnp.int32(0), 2 - (near == 1), jnp.int32(4)]
    meta = jnp.concatenate(
        [place[0] + steps, prod_place - 8 * group, prod_place + steps, jnp.stack(order + [group, near])]
    ).astype(jnp.int32)

    yes = jnp.bool_(True)
    own_table = table_of(
        dest_of([(0, group ^ bits, yes) for bits in range(4)], lambda delta: 0)
        + [group ^ bits for bits in range(4)] + valid_of(0),
        [threshold(0, 0)],
    )
    near_items = (oy, oy_core, dd, dd_core)
    near_table = table_of(
        dest_of(
            [(near, group, yes), (near, group ^ 1, yes), (near, group ^ 2, other), (near, group ^ 3, other)],
            lambda delta: 0,
        )
        + valid_of(near),
        [threshold(near, "near")],
    )
    far_items = (za, zb, z_core, bx, bx_core, by_0, by_0_core, by_1, by_1_core, dd, dd_core)
    far_dest = dest_of(
        [
            (-2 * sign, group, yes),
            (2 * sign, group, yes),
            (jnp.where((group == 0) | (group == 2), -2, 2), group ^ 1, yes),
            (2 * sign, group ^ 2, yes),
            (2 * sign, group ^ 3, yes),
            (-near, group, yes),
            (-near, group ^ 1, yes),
            (-near, group, yes),
            (-near, group ^ 1, yes),
            (-near, group ^ 2, same),
            (-near, group ^ 3, same),
        ],
        lambda delta: jnp.where(delta == -2, 1, jnp.where(delta == 2, 2, 0)),
    )
    far_table = table_of(
        far_dest + valid_of(-near) + valid_of(-2) + valid_of(2),
        [threshold(-near, "far"), threshold(-2, -2), threshold(2, 2)],
    )

    smem = pl.BlockSpec(memory_space=pltpu.SMEM)
    vmem = pl.BlockSpec(memory_space=pltpu.VMEM)
    hbm = pl.BlockSpec(memory_space=pltpu.HBM)
    shards = (row_count, block, width)
    rows, depth, columns = row_count * block, WINDOWS * 8 * block, 16 * block
    shape = jax.ShapeDtypeStruct
    bf16, f32 = jnp.bfloat16, jnp.float32

    small = pltpu.CompilerParams(vmem_limit_bytes=22 << 20)

    def cost(k):
        return pl.CostEstimate(flops=2 * rows * k * columns * 2, bytes_accessed=12 << 20, transcendentals=0)

    def in_hbm(*values):
        return [pltpu.with_memory_space_constraint(value, pltpu.HBM) for value in values]

    dma = pltpu.SemaphoreType.DMA
    left_near, left_far_0, left_far_1, table_own, total = pl.pallas_call(
        own_kernel,
        out_shape=(
            pltpu.HBM((rows, 512), bf16),
            pltpu.HBM((rows // 2, 1536), bf16),
            pltpu.HBM((rows // 2, 1536), bf16),
            pltpu.HBM((512, columns), bf16),
            pltpu.HBM((rows, columns), f32),
        ),
        in_specs=[smem, smem] + [hbm] * 4,
        out_specs=(hbm,) * 5,
        scratch_shapes=[
            pltpu.VMEM((ka_count,) + shards, bf16),
            pltpu.VMEM((rows, 512), bf16),
            pltpu.VMEM((rows, 512), bf16),
            pltpu.VMEM((rows, 1536), bf16),
            pltpu.VMEM((PIECES,) + shards, bf16),
            pltpu.VMEM((512, columns), bf16),
            pltpu.VMEM((rows, columns), f32),
            dma((4,)),
            dma((5,)),
        ],
        compiler_params=small,
        cost_estimate=cost(512),
    )(meta, own_table, *in_hbm(own), own_core, *in_hbm(ox), ox_core)

    table_near, base_0, base_1 = pl.pallas_call(
        near_kernel,
        out_shape=(
            pltpu.HBM((512, columns), bf16),
            pltpu.HBM((row_count // 2, block, width), f32),
            pltpu.HBM((row_count // 2, block, width), f32),
        ),
        in_specs=[smem, smem] + [hbm] * 6,
        out_specs=(hbm, hbm, hbm),
        scratch_shapes=[
            pltpu.VMEM((PIECES,) + shards, bf16),
            pltpu.VMEM((rows, 512), bf16),
            pltpu.VMEM((rows, columns), f32),
            pltpu.VMEM((512, columns), bf16),
            pltpu.VMEM((rows, columns), f32),
            pltpu.VMEM(shards, f32),
            dma((4,)),
            dma((2,)),
            dma((3,)),
        ],
        compiler_params=small,
        cost_estimate=cost(512),
    )(meta, near_table, *in_hbm(left_near, total, *near_items))

    half_rows = row_count // 2
    half_shape = (half_rows, block, width)
    table_b, square_0, low_0 = pl.pallas_call(
        far_kernel,
        out_shape=(shape((1536, columns), bf16), shape(half_shape, f32), shape(half_shape, bf16)),
        in_specs=[smem, smem, vmem, vmem, hbm, hbm] + [vmem] * 7 + [hbm, hbm],
        out_specs=(vmem, vmem, vmem),
        scratch_shapes=[
            pltpu.VMEM((3 * PIECES, row_count, block, width), bf16),
            pltpu.VMEM((rows // 2, columns), f32),
            dma((4,)),
        ],
        compiler_params=small,
        cost_estimate=cost(1536),
    )(meta, far_table, *in_hbm(left_far_0, base_0, za, zb), *far_items[2:9], *in_hbm(dd, dd_core))
    square_1, low_1 = pl.pallas_call(
        second_kernel,
        out_shape=(shape(half_shape, f32), shape(half_shape, bf16)),
        in_specs=[smem] + [vmem] * 3,
        out_specs=(vmem, vmem),
        scratch_shapes=[pltpu.VMEM((rows // 2, columns), f32)],
        compiler_params=small,
        cost_estimate=cost(768),
    )(meta, *in_hbm(left_far_1, base_1), table_b)

    lows, square = (low_0, low_1), (square_0, square_1)
    by_x = [permuted(low, route["x"]) for low in lows]
    by_partner = [permuted(low, route["core"]) for low in lows]
    by_both = [permuted(low, route["core"]) for low in by_x]
    out = ()
    for part in range(2):
        out = (pl.pallas_call(
            functools.partial(cube_kernel, part),
            out_shape=pltpu.HBM((row_count, block, width), bf16),
            in_specs=[smem] + [vmem] * 8 + [hbm] * part,
            out_specs=hbm,
            scratch_shapes=[
                pltpu.VMEM((ka_count, half_rows, block, width), bf16),
                pltpu.VMEM((rows // 2, depth), bf16),
                pltpu.VMEM((rows // 2, columns), f32),
                pltpu.VMEM((half_rows, block, width), bf16),
                pltpu.SemaphoreType.DMA,
            ],
            input_output_aliases={9: 0} if part else {},
            compiler_params=small,
            cost_estimate=cost(1280),
        )(meta, lows[part], by_partner[part], by_x[part], by_both[part],
          table_own, table_near, table_b, square[part], *out),)
    return out[0]


def solution(mesh):
    def body(*args):
        return per_device(mesh.shape["dom"], mesh.shape["ka"], *args)

    return jax.shard_map(
        body,
        mesh=mesh,
        in_specs=(P("dom", None, "ka"), P("dom", None), P("dom", None)),
        out_specs=P("dom", None, "ka"),
        check_vma=False,
    )
```
